128 devices in a mesh: kv: 2 (over y_lo), ctx: 64 (over z, x, y_hi, core).
Axes of the slice: x: 4, y: 4 (y_hi: 2, y_lo: 2; y = y_hi * 2 + y_lo), z: 4, core: 2. Of those that a mesh axis runs over, the one named last changes fastest.
Arguments:
- residual: bfloat16 [64, 8192], P(None, 'ctx'), may hold values from -8 to 8
- queries: bfloat16 [64, 8192], P(None, 'kv'), may hold values from -16 to 16
- draft_token_keys: bfloat16 [64, 1024], P(None, 'kv'), may hold values from -32 to 32
- draft_token_values: bfloat16 [64, 1024], P(None, 'kv'), may hold values from -8 to 8
- cache_keys: bfloat16 [2, 32768, 1024], P(None, 'ctx', 'kv'), may hold values from -32 to 32
- cached_value_rows: bfloat16 [2, 32768, 1024], P(None, 'ctx', 'kv'), may hold values from -8 to 8
- tenant_ids: int32 [64], replicated, may hold values from 0 to 1, as said below
- tree_mask: int32 [64, 64], replicated, may hold values from 0 to 1, as said below
- cache_lengths: int32 [2], replicated, may hold values from 16385 to 32768
- out_weight: bfloat16 [8192, 8192], P('kv', 'ctx'), may hold values from -0.0625 to 0.0625
- out_signs: bfloat16 [2, 8192, 8192], P(None, 'kv', 'ctx'), may hold values from -1 to 1, as said below
- norm_gain: float32 [8192], P('ctx'), may hold values from 0.1 to 1.9
- gate_weight: bfloat16 [8192, 16384], P(None, ('kv', 'ctx')), may hold values from -0.0625 to 0.0625
- up_weight: bfloat16 [8192, 16384], P(None, ('kv', 'ctx')), may hold values from -0.0625 to 0.0625
- down_weight: bfloat16 [16384, 8192], P(('kv', 'ctx')), may hold values from -0.1875 to 0.1875
- gate_signs: bfloat16 [2, 8192, 16384], P(None, None, ('kv', 'ctx')), may hold values from -1 to 1, as said below
- up_signs: bfloat16 [2, 8192, 16384], P(None, None, ('kv', 'ctx')), may hold values from -1 to 1, as said below
- down_signs: bfloat16 [2, 16384, 8192], P(None, ('kv', 'ctx')), may hold values from -1 to 1, as said below
- delta_scale: float32 [2, 4], replicated, may hold values from 0.3 to 0.9
Outputs:
- mixed: bfloat16 [64, 8192], P(None, 'ctx')
The draws below stay inside these ranges and needn't reach their ends.
Inputs may be any that keep to these rules, and one draw needn't show every extreme that they name: `tenant_ids`: exactly 32 tokens belong to each tenant. `tree_mask`: entry (i, j) is 1 exactly when token j is token i or an ancestor of token i in the draft tree of their common tenant; each tenant's 32 tokens form one tree. `out_signs`: every entry is 1 or -1. `gate_signs`: every entry is 1 or -1. `up_signs`: every entry is 1 or -1. `down_signs`: every entry is 1 or -1.
All inputs are finite; a program needn't handle non-finite values.
Results may differ from the reference program's by a relative error of at most 0.013.
Values may be sent and summed in bfloat16 or wider, within the bound.
A program may use at most 128 MiB of HBM per device.

```python
import math
import jax
import jax.numpy as jnp
from jax import lax

D = 8192
QUERY_HEADS = 64
KEY_VALUE_HEADS = 8
HEAD_SIZE = 128
FF = 16384
TENANT_COUNT = 2
DRAFT_TOKENS = 32
ALL_TOKENS = 64
CACHE_SLOTS = 32768


def tree_parts(key):
    base_matrix = jax.random.fold_in(key, 7001)
    key_perm, key_parent = jax.random.split(base_matrix)
    shuffled = jax.random.permutation(key_perm, ALL_TOKENS).astype(jnp.int32)
    tenant_index = (shuffled // DRAFT_TOKENS).astype(jnp.int32)
    ranking = (shuffled % DRAFT_TOKENS).astype(jnp.int32)
    ranks = jnp.arange(DRAFT_TOKENS, dtype=jnp.int32)
    parent = jax.random.randint(key_parent, (TENANT_COUNT, DRAFT_TOKENS), 0, jnp.maximum(ranks, 1))
    parent_links = ((parent[:, :, None] == ranks[None, None, :]) & (ranks[None, :, None] > 0)).astype(jnp.int32)
    identity_matrix = jnp.broadcast_to(jnp.eye(DRAFT_TOKENS, dtype=jnp.int32), (TENANT_COUNT, DRAFT_TOKENS, DRAFT_TOKENS))

    def extend(step, reachable):
        return jnp.minimum(identity_matrix + jnp.einsum('dnv,dvo->dno', parent_links, reachable), 1)
    reachable = lax.fori_loop(0, DRAFT_TOKENS, extend, identity_matrix)
    same_tenant = (tenant_index[:, None] == tenant_index[None, :]).astype(jnp.int32)
    ancestry = reachable[tenant_index[:, None], ranking[:, None], ranking[None, :]] * same_tenant
    return (tenant_index, ancestry.astype(jnp.int32))


def draw_tenant_ids(key, part):
    return tree_parts(key)[0]


def draw_tree_mask(key, part):
    return tree_parts(key)[1]


def jitter_sample(key, shape):
    return jnp.clip(jax.random.normal(key, shape, jnp.float32), -4.0, 4.0)


def query_parts(key):
    base_matrix = jax.random.fold_in(key, 7002)
    key_common, key_own, key_jitter = jax.random.split(base_matrix, 3)
    tenant_index = tree_parts(key)[0]
    group_width = QUERY_HEADS // KEY_VALUE_HEADS
    common = jitter_sample(key_common, (TENANT_COUNT, QUERY_HEADS, HEAD_SIZE))
    own = jitter_sample(key_own, (ALL_TOKENS, QUERY_HEADS, HEAD_SIZE))
    additional = jitter_sample(key_jitter, (ALL_TOKENS, KEY_VALUE_HEADS, HEAD_SIZE))
    shared_part = common[tenant_index]
    query_matrix = 2.5 * (0.7 * shared_part + 0.71 * own)
    draft_key_matrix = 0.32 * 1.75 * shared_part.reshape(ALL_TOKENS, KEY_VALUE_HEADS, group_width, HEAD_SIZE).sum(axis=2) + 0.3 * additional
    return (query_matrix.reshape(ALL_TOKENS, QUERY_HEADS * HEAD_SIZE), draft_key_matrix.reshape(ALL_TOKENS, KEY_VALUE_HEADS * HEAD_SIZE))


def draw_queries(key, part):
    return query_parts(key)[0].astype(jnp.bfloat16)


def draw_draft_token_keys(key, part):
    return query_parts(key)[1].astype(jnp.bfloat16)


def draw_cache_keys(key, part):
    base_matrix = jax.random.fold_in(key, 7004)
    tenant_cache = jitter_sample(base_matrix, (TENANT_COUNT, CACHE_SLOTS, KEY_VALUE_HEADS * HEAD_SIZE))
    return tenant_cache.astype(jnp.bfloat16)


def draw_residual(key, part):
    base_matrix = jax.random.fold_in(key, 7005)
    ramp = jnp.arange(D, dtype=jnp.float32) / D
    values = jnp.clip(jax.random.normal(base_matrix, (ALL_TOKENS, D), jnp.float32), -4.0, 4.0) * (0.6 + 1.2 * ramp)
    return values.astype(jnp.bfloat16)


def sign_draw(key, salt, shape):
    flips = jax.random.bernoulli(jax.random.fold_in(key, salt), 0.5, shape)
    return jnp.where(flips, 1.0, -1.0).astype(jnp.float32).astype(jnp.bfloat16)


def draw_out_signs(key, part):
    return sign_draw(key, 7011, (TENANT_COUNT, QUERY_HEADS * HEAD_SIZE, D))


def draw_gate_signs(key, part):
    return sign_draw(key, 7012, (TENANT_COUNT, D, FF))


def draw_up_signs(key, part):
    return sign_draw(key, 7013, (TENANT_COUNT, D, FF))


def draw_down_signs(key, part):
    return sign_draw(key, 7014, (TENANT_COUNT, FF, D))


def with_spikes(values, own_key, source, target, shards_of, factor):
    def block_of(position):
        return (jnp.arange(values.shape[position]) // (values.shape[position] // shards_of)).reshape((-1,) + (1,) * (values.ndim - 1 - position))

    near = jax.random.permutation(own_key, shards_of)[block_of(target)]
    other_side = (block_of(target) + shards_of // 2) % shards_of
    return jnp.where((block_of(source) == near) | (block_of(source) == other_side), factor * values, values)


def block_scale(own_key, dims, cuts, least, top_value):
    gain, own = 1.0, jax.random.fold_in(own_key, 6)
    for position, blocks in cuts:
        heights = jnp.exp(jax.random.uniform(jax.random.fold_in(own, position), (blocks,), jnp.float32, least / len(cuts), top_value / len(cuts)))
        gain = gain * jnp.repeat(heights, dims[position] // blocks).reshape([-1 if axis == position else 1 for axis in range(len(dims))])
    return gain


def bell_draw(rng, extent, width, most, cuts=(), held_as=jnp.bfloat16):
    factor_of = block_scale(rng, extent, cuts, -0.22, 0.18) if cuts else 1.0
    drawn = jax.random.normal(rng, extent, jnp.float32) * width * factor_of
    return jnp.minimum(jnp.maximum(drawn, -most), most).astype(held_as)


def noise_with(own_key, dims, scale, bound, shards, heavy, kind=jnp.bfloat16):
    values = scale * jax.random.normal(own_key, dims, jnp.float32)
    if shards:
        values = values * block_scale(own_key, dims, shards, -0.22, 0.18)
    return jnp.clip(with_spikes(values, jax.random.fold_in(own_key, 3), *heavy), -bound, bound).astype(kind)


def setup_inputs(seed: int = 0) -> dict:
    streams_of = jax.random.split(jax.random.key(seed), 20)
    residual = draw_residual(jax.random.fold_in(streams_of[19], 71), 0)
    queries = draw_queries(jax.random.fold_in(streams_of[19], 71), 0)
    draft_token_keys = draw_draft_token_keys(jax.random.fold_in(streams_of[19], 71), 0)
    draft_token_values = bell_draw(streams_of[3], (ALL_TOKENS, KEY_VALUE_HEADS * HEAD_SIZE), 2.0, 8.0, ((1, 2),))
    cache_keys = draw_cache_keys(jax.random.fold_in(streams_of[19], 71), 0)
    cached_value_rows = bell_draw(streams_of[5], (TENANT_COUNT, CACHE_SLOTS, KEY_VALUE_HEADS * HEAD_SIZE), 2.0, 8.0, ((1, 64), (2, 2)))
    tenant_ids = draw_tenant_ids(jax.random.fold_in(streams_of[19], 71), 0)
    tree_mask = draw_tree_mask(jax.random.fold_in(streams_of[19], 71), 0)
    cache_lengths = jax.random.randint(streams_of[8], (TENANT_COUNT,), CACHE_SLOTS // 2 + 1, CACHE_SLOTS + 1).astype(jnp.int32)
    out_weight = bell_draw(streams_of[9], (QUERY_HEADS * HEAD_SIZE, D), (QUERY_HEADS * HEAD_SIZE) ** -0.5, 0.0625, ((0, 2), (1, 64)))
    out_signs = draw_out_signs(jax.random.fold_in(streams_of[19], 71), 0)
    norm_gain = jnp.clip(1.0 + 0.18 * jax.random.normal(streams_of[11], (D,), jnp.float32), 0.1, 1.9)
    gate_weight = bell_draw(streams_of[12], (D, FF), D ** -0.5, 0.0625, ((1, 128),))
    up_weight = bell_draw(streams_of[13], (D, FF), D ** -0.5, 0.0625, ((1, 128),))
    down_weight = noise_with(streams_of[14], (FF, D), FF ** -0.5, 0.1875, ((0, 128),), (0, 1, 128, 5.5))
    gate_signs = draw_gate_signs(jax.random.fold_in(streams_of[19], 71), 0)
    up_signs = draw_up_signs(jax.random.fold_in(streams_of[19], 71), 0)
    down_signs = draw_down_signs(jax.random.fold_in(streams_of[19], 71), 0)
    delta_scale = jnp.clip(jnp.exp(jax.random.uniform(streams_of[18], (TENANT_COUNT, 4), jnp.float32, math.log(0.3), math.log(0.9))), 0.3, 0.9)
    return dict(residual=residual, queries=queries, draft_token_keys=draft_token_keys, draft_token_values=draft_token_values, cache_keys=cache_keys, cached_value_rows=cached_value_rows, tenant_ids=tenant_ids, tree_mask=tree_mask, cache_lengths=cache_lengths, out_weight=out_weight, out_signs=out_signs, norm_gain=norm_gain, gate_weight=gate_weight, up_weight=up_weight, down_weight=down_weight, gate_signs=gate_signs, up_signs=up_signs, down_signs=down_signs, delta_scale=delta_scale)


NEG = -1e+30
EPS = 1e-05

def tenant_products(inputs, signs, factor):
    results = []
    for tenant_index in range(TENANT_COUNT):
        block_rows = inputs[tenant_index * DRAFT_TOKENS:(tenant_index + 1) * DRAFT_TOKENS]
        product = jnp.dot(block_rows, signs[tenant_index], preferred_element_type=jnp.float32)
        results.append(product * factor[tenant_index])
    return jnp.concatenate(results, axis=0)

def reference(residual, queries, draft_token_keys, draft_token_values, cache_keys, cached_value_rows, tenant_ids, tree_mask, cache_lengths, out_weight, out_signs, norm_gain, gate_weight, up_weight, down_weight, gate_signs, up_signs, down_signs, delta_scale):
    sort_order = jnp.argsort(tenant_ids, stable=True).astype(jnp.int32)
    inverse = jnp.argsort(sort_order).astype(jnp.int32)
    group_width = QUERY_HEADS // KEY_VALUE_HEADS
    factor = HEAD_SIZE ** (-0.5)
    ordered_queries = queries[sort_order].astype(jnp.float32).reshape(TENANT_COUNT, DRAFT_TOKENS, KEY_VALUE_HEADS, group_width, HEAD_SIZE)
    draft_key_lines = draft_token_keys[sort_order].astype(jnp.float32).reshape(ALL_TOKENS, KEY_VALUE_HEADS, HEAD_SIZE)
    draft_value_lines = draft_token_values[sort_order].astype(jnp.float32).reshape(ALL_TOKENS, KEY_VALUE_HEADS, HEAD_SIZE)
    visible = (tree_mask[sort_order][:, sort_order] > 0).reshape(TENANT_COUNT, DRAFT_TOKENS, 1, ALL_TOKENS)
    live = (jnp.arange(CACHE_SLOTS, dtype=jnp.int32)[None, :] < cache_lengths[:, None])[:, None, None, :]

    def single_group(index):
        query_part = lax.dynamic_index_in_dim(ordered_queries, index, 2, keepdims=False)
        keys_cache = lax.dynamic_slice_in_dim(cache_keys, index * HEAD_SIZE, HEAD_SIZE, 2).astype(jnp.float32)
        values_cache = lax.dynamic_slice_in_dim(cached_value_rows, index * HEAD_SIZE, HEAD_SIZE, 2).astype(jnp.float32)
        keys_draft = lax.dynamic_index_in_dim(draft_key_lines, index, 1, keepdims=False)
        values_draft = lax.dynamic_index_in_dim(draft_value_lines, index, 1, keepdims=False)
        cache_scores = jnp.einsum('tqwd,tjd->tqwj', query_part, keys_cache) * factor
        draft_scores = jnp.einsum('tqwd,kd->tqwk', query_part, keys_draft) * factor
        cache_masked = jnp.where(live, cache_scores, NEG)
        draft_masked = jnp.where(visible, draft_scores, NEG)
        peak = jnp.maximum(lax.optimization_barrier(jnp.max(cache_masked, axis=-1)), lax.optimization_barrier(jnp.max(draft_masked, axis=-1)))
        cache_weights = jnp.where(live, jnp.exp(cache_masked - peak[..., None]), 0.0)
        draft_weights = jnp.where(visible, jnp.exp(draft_masked - peak[..., None]), 0.0)
        total = lax.optimization_barrier(jnp.sum(cache_weights, axis=-1)) + lax.optimization_barrier(jnp.sum(draft_weights, axis=-1))
        cache_rounded = lax.optimization_barrier(cache_weights.astype(jnp.bfloat16)).astype(jnp.float32)
        draft_rounded = lax.optimization_barrier(draft_weights.astype(jnp.bfloat16)).astype(jnp.float32)
        combined = jnp.einsum('tqwj,tjd->tqwd', cache_rounded, values_cache)
        combined = combined + jnp.einsum('tqwk,kd->tqwd', draft_rounded, values_draft)
        return (combined / total[..., None]).astype(jnp.bfloat16)
    group_share = lax.map(single_group, jnp.arange(KEY_VALUE_HEADS, dtype=jnp.int32))
    attention = jnp.transpose(group_share, (1, 2, 0, 3, 4)).reshape(ALL_TOKENS, QUERY_HEADS * HEAD_SIZE)
    scales = delta_scale.astype(jnp.float32)
    projected = jnp.dot(attention, out_weight, preferred_element_type=jnp.float32)
    projected = projected + tenant_products(attention, out_signs, scales[:, 0] * (QUERY_HEADS * HEAD_SIZE) ** (-0.5))
    hidden = residual[sort_order].astype(jnp.float32) + projected
    normed = (hidden * lax.rsqrt(lax.optimization_barrier(jnp.mean(hidden * hidden, axis=1)) + EPS)[:, None] * norm_gain).astype(jnp.bfloat16)
    gate = jnp.dot(normed, gate_weight, preferred_element_type=jnp.float32)
    gate = gate + tenant_products(normed, gate_signs, scales[:, 1] * D ** (-0.5))
    up_part = jnp.dot(normed, up_weight, preferred_element_type=jnp.float32)
    up_part = up_part + tenant_products(normed, up_signs, scales[:, 2] * D ** (-0.5))
    active = (jax.nn.silu(gate) * up_part).astype(jnp.bfloat16)
    lowered = jnp.dot(active, down_weight, preferred_element_type=jnp.float32)
    lowered = lowered + tenant_products(active, down_signs, scales[:, 3] * FF ** (-0.5))
    return (hidden + lowered).astype(jnp.bfloat16)[inverse]
```

```python
import functools

import jax
import jax.numpy as jnp
from jax import lax
from jax.experimental import pallas as pl
from jax.experimental.pallas import tpu as pltpu
from jax.sharding import PartitionSpec as P

D = 8192
FF = 16384
HEAD = 128
SLOTS = 512
NEG = -1e30
EPS = 1e-05
MESH = pl.DeviceIdType.MESH
f32, bf16, i32 = jnp.float32, jnp.bfloat16, jnp.int32
ORDER = (2, 1, 3)
NEAR = (1, 3, 2)


def dot(a, b, dims=((1,), (0,))):
    return lax.dot_general(a, b, (dims, ((), ())), preferred_element_type=f32)


def mult(v, n):
    return pl.multiple_of(v, n)


def lanes():
    return lax.broadcasted_iota(i32, (32, 128), 1)


def split(st):
    hi = st.astype(bf16).astype(f32)
    mid = (st - hi).astype(bf16).astype(f32)
    lo = st - hi - mid
    lane = lanes()
    return jnp.where(
        lane < 32, hi, jnp.where(lane < 64, mid, jnp.where(lane < 96, lo, 0.0))
    ).astype(bf16)


def join(block):
    v = block.astype(f32)
    v = v + pltpu.roll(v, 32, 1)
    return v + pltpu.roll(v, 64, 1)


def blend(stats):
    top = functools.reduce(jnp.maximum, stats)
    parts = [jnp.exp(s - top) for s in stats]
    total = functools.reduce(jnp.add, parts)
    inverse = 1.0 / total
    return [w * inverse for w in parts], top + jnp.log(total)


def mixed_of(factors, blocks, k):
    terms = [f[:, k : k + 1] * b for f, b in zip(factors, blocks)]
    return functools.reduce(jnp.add, terms)


def layer(
    ids_h, mask_h, lens, dsc, res_h, q_h, dk_h, dv_h, ck_h, cv_h, wo_h, so_h, gain_h,
    wg_h, wu_h, wd_h, sg_h, su_h, sd_h,
    out_ref,
    ids, mask, qraw, qs, kc, vc, dk, dv, vis, pm, pt, wo, so, wg, wu, wd, sg, su, sd,
    rres, gains, acs, acr, a1s, a1r, a2s, a2r, a3s, a3r, ab, yb, hid, gb, ss,
    ecs, ecr, e1o, e1s, e1r, e2s, e2r, e3s, e3r,
    ls, c_s, c_r, a1_s, a1_r, a2_s, a2_r, a3_s, a3_r, r_s, r_r,
    bq_s, bq_r, bp_s, bp_r, bc_s, bc_r, y_s, y_r,
    dq_s, dq_r, dp_s, dp_r, dc_s, dc_r, n_s, n_r,
    e0_s, e0_r, e1_s, e1_r, e2_s, e2_r, e3_s, e3_r,
):
    kv, ctx = lax.axis_index("kv"), lax.axis_index("ctx")
    c = ctx % 2
    yh = (ctx // 2) % 2
    x = (ctx // 4) % 4
    z = ctx // 16
    p = z + c * (x - z)
    q = x + c * (z - x)
    sp, sq = 16 - 12 * c, 4 + 12 * c
    yi = yh * 2 + kv
    oc = 1 - c

    core = (kv, ctx + 1 - 2 * c)

    def p_dev(d):
        return (kv, ctx + ((p + d) % 4 - p) * sp)

    def q_dev(d):
        return (kv, ctx + ((q + d) % 4 - q) * sq)

    def y_dev(d):
        to = (yi + d) % 4
        return (to % 2, ctx + (to // 2 - yh) * 2)

    far = (kv, ctx + 2 - 4 * yh)
    near_step = 3 - 2 * (yi % 2)
    near = y_dev(near_step)

    barrier = pltpu.get_barrier_semaphore()
    peers = [core] + [p_dev(d) for d in NEAR] + [q_dev(d) for d in NEAR] + [y_dev(d) for d in NEAR]
    for peer in peers:
        pl.semaphore_signal(barrier, inc=1, device_id=peer, device_id_type=MESH)

    def load(n, src, dst):
        copy = pltpu.make_async_copy(src, dst, ls.at[n])
        copy.start()
        return copy

    first = [load(0, ids_h, ids), load(1, q_h, qraw)]
    other_keys = load(2, ck_h.at[oc], kc.at[oc])
    other_values = load(3, cv_h.at[oc], vc.at[oc])
    own_keys = load(4, ck_h.at[c], kc.at[c])
    own_values = load(5, cv_h.at[c], vc.at[c])
    small = [
        load(6, mask_h, mask), load(7, dk_h, dk), load(8, dv_h, dv),
        load(9, res_h, rres.at[yh]), load(10, gain_h, gains.at[yh]),
    ]

    sent = []

    def send(src, dst, s_sem, r_sem, to):
        copy = pltpu.make_async_remote_copy(
            src_ref=src, dst_ref=dst, send_sem=s_sem, recv_sem=r_sem,
            device_id=to, device_id_type=MESH,
        )
        copy.start()
        sent.append((src, s_sem))

    def arrived(dst, sem):
        pltpu.make_async_copy(dst, dst, sem).wait()

    for copy in first:
        copy.wait()
    row = jnp.broadcast_to(ids[...].astype(f32), (64, 64))
    ii = lax.broadcasted_iota(i32, (64, 64), 0)
    jj = lax.broadcasted_iota(i32, (64, 64), 1)
    col = jnp.sum(jnp.where(ii == jj, row, 0.0), axis=1, keepdims=True)
    same = jnp.where(row == col, 1.0, 0.0)
    pos_col = jnp.sum(jnp.where(jj < ii, same, 0.0), axis=1, keepdims=True) + 32.0 * col
    pos_row = jnp.sum(jnp.where(ii < jj, same, 0.0), axis=0, keepdims=True) + 32.0 * row[:1]
    pt[...] = jnp.where(pos_col == jj.astype(f32), 1.0, 0.0).astype(bf16)
    pm[...] = jnp.where(pos_row == ii.astype(f32), 1.0, 0.0).astype(bf16)

    @pl.loop(0, 4)
    def _(n):
        at = pl.ds(mult(n * 1024, 1024), 1024)
        qs[:, at] = dot(pm[...], qraw[:, at]).astype(bf16)

    factor = HEAD ** (-0.5)
    c32, o32 = mult(c * 32, 32), mult(oc * 32, 32)
    first_slot = ctx * SLOTS

    def attend(t, t32, g):
        rows = jnp.concatenate(
            [qs[pl.ds(t32, 32), pl.ds(mult((g * 8 + k) * 128, 128), 128)] for k in range(8)], axis=0
        )
        at = pl.ds(mult(g * 128, 128), 128)
        s = dot(rows, kc[t, :, at], ((1,), (1,))) * factor
        live = lax.broadcasted_iota(i32, (1, SLOTS), 1) + first_slot < lens[t]
        s = jnp.where(live, s, NEG)
        m = jnp.max(s, axis=1, keepdims=True)
        e = jnp.where(live, jnp.exp(s - m), 0.0)
        l = jnp.sum(e, axis=1, keepdims=True)
        o = dot(e.astype(bf16), vc[t, :, at])
        some = l > 0.0
        safe = jnp.where(some, l, 1.0)
        o = o * (1.0 / safe)
        lse = jnp.where(some, m + jnp.log(safe), NEG)
        lane = lanes() % 32
        st = jnp.zeros((32, 128), f32)
        for k in range(8):
            st = jnp.where(lane == k, lse[k * 32 : (k + 1) * 32], st)
        return o, st

    other_keys.wait()
    other_values.wait()
    rest = [
        load(11, wo_h, wo), load(12, so_h, so), load(13, wg_h, wg), load(14, wu_h, wu),
        load(15, sg_h, sg), load(16, su_h, su), load(17, wd_h, wd), load(18, sd_h, sd),
    ]
    pl.semaphore_wait(barrier, len(peers))

    def offset(i):
        return 2 - i + 3 * (i // 2) - 2 * (i // 3)

    @pl.loop(0, 4)
    def _(i):
        d = offset(i)
        o, st = attend(oc, o32, (q + d) % 4)
        for k in range(8):
            acs[d, k] = o[k * 32 : (k + 1) * 32].astype(bf16)
        acs[d, 8] = split(st)
        pltpu.make_async_remote_copy(
            src_ref=acs.at[d], dst_ref=acr.at[d], send_sem=c_s.at[d], recv_sem=c_r.at[d],
            device_id=core, device_id_type=MESH,
        ).start()

    own_keys.wait()
    own_values.wait()
    for copy in small:
        copy.wait()
    send(rres.at[yh], rres.at[yh], r_s.at[0], r_r.at[0], near)
    send(gains.at[yh], gains.at[yh], r_s.at[1], r_r.at[1], near)

    @pl.loop(0, 4)
    def _(i):
        d = offset(i)
        o, st = attend(c, c32, (p + d) % 4)
        arrived(acr.at[d], c_r.at[d])
        factors, lse = blend([st, join(acr[d, 8])])
        for k in range(8):
            blocks = [o[k * 32 : (k + 1) * 32], acr[d, k].astype(f32)]
            a1s[d, k] = mixed_of(factors, blocks, k).astype(bf16)
        a1s[d, 8] = split(lse)

        @pl.when(d != 0)
        def _():
            pltpu.make_async_remote_copy(
                src_ref=a1s.at[d], dst_ref=a1r.at[d - 1], send_sem=a1_s.at[d - 1],
                recv_sem=a1_r.at[d - 1], device_id=p_dev(d), device_id_type=MESH,
            ).start()

    for d in range(4):
        sent.append((acs.at[d], c_s.at[d]))
    for d in ORDER:
        sent.append((a1s.at[d], a1_s.at[d - 1]))

    vis[...] = dot(pm[...], mask[...].astype(f32).astype(bf16))
    head0 = p * 8 + q * 2
    rows = jnp.concatenate(
        [qs[pl.ds(c32, 32), pl.ds(mult((head0 + k) * 128, 128), 128)] for k in range(2)], axis=0
    )
    at_p = pl.ds(mult(p * 128, 128), 128)
    seen = jnp.concatenate([vis[pl.ds(c32, 32), :]] * 2, axis=0) > 0.5
    s = jnp.where(seen, dot(rows, dk[:, at_p], ((1,), (1,))) * factor, NEG)
    m = jnp.max(s, axis=1, keepdims=True)
    e = jnp.where(seen, jnp.exp(s - m), 0.0)
    l = jnp.sum(e, axis=1, keepdims=True)
    draft_o = dot(e.astype(bf16), dv[:, at_p]) * (1.0 / l)
    lse = m + jnp.log(l)
    draft_st = jnp.where(lanes() % 32 == 0, lse[:32], lse[32:])

    for d in NEAR:
        arrived(a1r.at[d - 1], a1_r.at[d - 1])
    sources = [a1s.at[0]] + [a1r.at[n] for n in range(3)]
    factors, lse = blend([join(s[8]) for s in sources])
    keep = None
    for d in ORDER + (0,):
        to_q = (q + d) % 4
        shift = (128 - 2 * to_q) % 128
        turned = [pltpu.roll(f, shift, 1) for f in factors]
        heads = [
            mixed_of(turned, [s[2 * to_q + k].astype(f32) for s in sources], k) for k in range(2)
        ]
        st = pltpu.roll(lse, shift, 1)
        if d:
            a2s[d, 0] = heads[0].astype(bf16)
            a2s[d, 1] = heads[1].astype(bf16)
            a2s[d, 2] = split(st)
            send(a2s.at[d], a2r.at[d - 1], a2_s.at[d - 1], a2_r.at[d - 1], q_dev(d))
        else:
            keep = (heads, st)

    for d in NEAR:
        arrived(a2r.at[d - 1], a2_r.at[d - 1])
    factors, lse = blend([keep[1]] + [join(a2r[n, 2]) for n in range(3)])
    heads = [
        mixed_of(factors, [keep[0][k]] + [a2r[n, k].astype(f32) for n in range(3)], k)
        for k in range(2)
    ]
    a3s[0] = heads[0].astype(bf16)
    a3s[1] = heads[1].astype(bf16)
    a3s[2] = split(lse)
    send(a3s, a3r, a3_s.at[0], a3_r.at[0], far)
    arrived(a3r, a3_r.at[0])
    factors, _ = blend([lse, join(a3r[2]), draft_st])
    for k in range(2):
        blocks = [heads[k], a3r[k].astype(f32), draft_o[k * 32 : (k + 1) * 32]]
        ab[c, p, q, :, k * 128 : (k + 1) * 128] = mixed_of(factors, blocks, k).astype(bf16)

    def gather(buf, q_s, q_r, p_s, p_r, k_s, k_r, ring):
        def unit(dp, dq):
            return buf.at[c, (p - dp + 4) % 4, (q - dq + 4) % 4]

        def theirs(dp, dq):
            return buf.at[oc, (q - dp + 4) % 4, (p - dq + 4) % 4]

        def to_core(dp, dq):
            at = unit(dp, dq)
            send(at, at, k_s.at[dp, dq], k_r.at[dp, dq], core)

        def to_p(dq):
            at = unit(0, dq)
            for d in ORDER:
                send(at, at, p_s.at[d - 1, dq], p_r.at[d - 1, dq], p_dev(d))

        at = unit(0, 0)
        for d in ORDER:
            send(at, at, q_s.at[d - 1], q_r.at[d - 1], q_dev(d))
        to_p(0)
        to_core(0, 0)
        for dq in NEAR:
            arrived(unit(0, dq), q_r.at[dq - 1])
            to_p(dq)
            to_core(0, dq)

        def own_batch(dp):
            if dp:
                for dq in (0,) + NEAR:
                    arrived(unit(dp, dq), p_r.at[dp - 1, dq])
                    to_core(dp, dq)
            ring(c, (p - dp + 4) % 4, True)

        def core_batch(dp):
            for dq in (0,) + NEAR:
                arrived(theirs(dp, dq), k_r.at[dp, dq])
            ring(oc, (q - dp + 4) % 4, False)

        own_batch(0)
        own_batch(1)
        core_batch(0)
        own_batch(3)
        core_batch(1)
        own_batch(2)
        core_batch(3)
        core_batch(2)

    rest[0].wait()
    rest[1].wait()
    partial = {True: None, False: None}

    def out_batch(t, at_p, mine):
        lhs = jnp.concatenate([ab[t, at_p, n] for n in range(4)], axis=1)
        at = pl.ds(mult(at_p * 1024, 1024), 1024)
        both = jnp.concatenate([wo[at, :], so[t, at, :]], axis=1)
        value = dot(lhs, both)
        partial[mine] = value if partial[mine] is None else partial[mine] + value

    gather(ab, bq_s, bq_r, bp_s, bp_r, bc_s, bc_r, out_batch)
    for mine, t, t32 in ((True, c, c32), (False, oc, o32)):
        value = partial[mine]
        value = value[:, :128] + (dsc[t, 0] * D ** (-0.5)) * value[:, 128:]
        yb[yi, pl.ds(t32, 32), :] = value.astype(bf16)

    for d in ORDER:
        send(yb.at[yi], yb.at[yi], y_s.at[d - 1], y_r.at[d - 1], y_dev(d))
    arrived(rres.at[1 - yh], r_r.at[0])
    arrived(gains.at[1 - yh], r_r.at[1])
    base = [dot(pm[...], rres[b]) for b in range(2)]
    for d in NEAR:
        arrived(yb.at[(yi - d + 4) % 4], y_r.at[d - 1])
    squares = jnp.zeros((64, 1), f32)
    for b in range(2):
        h = base[b] + (yb[2 * b].astype(f32) + yb[2 * b + 1].astype(f32))
        hid[b] = h
        gb[c, p, q, :, b * 128 : (b + 1) * 128] = (h * gains[b]).astype(bf16)
        squares = squares + jnp.sum(h * h, axis=1, keepdims=True)
    ss[0, :, 0:64] = jnp.sum(jnp.where(ii == jj, squares, 0.0), axis=0, keepdims=True)
    ss[0, :, 64:128] = jnp.zeros((1, 64), f32)
    for d in ORDER:
        send(ss.at[0], ss.at[d], n_s.at[d - 1], n_r.at[d - 1], q_dev(d))

    for n in range(2, 6):
        rest[n].wait()
    sums = [None, None, None]

    def up_batch(t, at_p, mine):
        tp, tq = (sp, sq) if mine else (sq, sp)
        lhs = jnp.concatenate([gb[t, at_p, n] for n in range(4)], axis=1)

        def rows(ref, *lead):
            parts = []
            for n in range(4):
                start = (at_p * tp + n * tq + t) * 128
                for b in range(2):
                    parts.append(ref[(*lead, pl.ds(mult(start + b * 256, 128), 128), slice(None))])
            return jnp.concatenate(parts, axis=0)

        values = [dot(lhs, jnp.concatenate([rows(wg), rows(wu)], axis=1))]
        for n in range(2):
            both = jnp.concatenate([rows(sg, n), rows(su, n)], axis=1)
            values.append(dot(lhs[n * 32 : (n + 1) * 32], both))
        for n in range(3):
            sums[n] = values[n] if sums[n] is None else sums[n] + values[n]

    gather(gb, dq_s, dq_r, dp_s, dp_r, dc_s, dc_r, up_batch)
    for d in NEAR:
        arrived(ss.at[d], n_r.at[d - 1])
    ss[4] = ss[0] + ss[1] + ss[2] + ss[3]
    for d in ORDER:
        send(ss.at[4], ss.at[4 + d], n_s.at[2 + d], n_r.at[2 + d], p_dev(d))
    for d in NEAR:
        arrived(ss.at[4 + d], n_r.at[2 + d])
    ss[8] = ss[4] + ss[5] + ss[6] + ss[7]
    send(ss.at[8], ss.at[9], n_s.at[6], n_r.at[6], core)
    arrived(ss.at[9], n_r.at[6])
    whole = (ss[8] + ss[9])[:, 0:64]
    total = jnp.sum(jnp.where(ii == jj, whole, 0.0), axis=1, keepdims=True)
    scale = lax.rsqrt(total * (1.0 / D) + EPS)

    def halves(n, at):
        return dsc[0, n] * at, dsc[1, n] * at

    g0, g1 = halves(1, D ** (-0.5))
    u0, u1 = halves(2, D ** (-0.5))
    gate_delta = jnp.concatenate([g0 * sums[1][:, :128], g1 * sums[2][:, :128]], axis=0)
    up_delta = jnp.concatenate([u0 * sums[1][:, 128:], u1 * sums[2][:, 128:]], axis=0)
    gate = (sums[0][:, :128] + gate_delta) * scale
    up = (sums[0][:, 128:] + up_delta) * scale
    active = (gate / (1.0 + jnp.exp(-gate)) * up).astype(bf16)

    rest[6].wait()
    rest[7].wait()
    d0, d1 = halves(3, FF ** (-0.5))

    def down(t, at_p, tp, n, tq):
        start = (at_p * tp + n * tq + t) * 128

        def cols(ref, *lead):
            return jnp.concatenate(
                [
                    ref[(*lead, slice(None), pl.ds(mult(start + b * 256, 128), 128))]
                    for b in range(2)
                ],
                axis=1,
            )

        value = dot(active, cols(wd))
        delta = [d0 * dot(active[:32], cols(sd, 0)), d1 * dot(active[32:], cols(sd, 1))]
        return value + jnp.concatenate(delta, axis=0)

    for d in ORDER + (0,):
        for n in range(4):
            ecs[d, n] = down(oc, (q + d) % 4, sq, n, sp).astype(bf16)
        send(ecs.at[d], ecr.at[d], e0_s.at[d], e0_r.at[d], core)
    for d in ORDER + (0,):
        mine = [down(c, (p + d) % 4, sp, n, sq) for n in range(4)]
        arrived(ecr.at[d], e0_r.at[d])
        for n in range(4):
            value = mine[n] + ecr[d, n].astype(f32)
            if d:
                e1s[d - 1, n] = value.astype(bf16)
            else:
                e1o[n] = value
        if d:
            send(e1s.at[d - 1], e1r.at[d - 1], e1_s.at[d - 1], e1_r.at[d - 1], p_dev(d))
    for d in NEAR:
        arrived(e1r.at[d - 1], e1_r.at[d - 1])
    kept = None
    for d in ORDER + (0,):
        n = (q + d) % 4
        value = e1o[n]
        for s in range(3):
            value = value + e1r[s, n].astype(f32)
        if d:
            e2s[d - 1] = value.astype(bf16)
            send(e2s.at[d - 1], e2r.at[d - 1], e2_s.at[d - 1], e2_r.at[d - 1], q_dev(d))
        else:
            kept = value
    for d in NEAR:
        arrived(e2r.at[d - 1], e2_r.at[d - 1])
        kept = kept + e2r[d - 1].astype(f32)
    for b in range(2):
        e3s[b] = kept[:, b * 128 : (b + 1) * 128].astype(bf16)
    for d in ORDER:
        to_block = ((yi + d) % 4) // 2
        send(e3s.at[to_block], e3r.at[yi], e3_s.at[d - 1], e3_r.at[d - 1], y_dev(d))
    e3r[yi] = e3s[yh]
    for d in NEAR:
        arrived(e3r.at[(yi - d + 4) % 4], e3_r.at[d - 1])
    lowered = (e3r[0].astype(f32) + e3r[1].astype(f32)) + (e3r[2].astype(f32) + e3r[3].astype(f32))
    result = (hid[yh] + lowered).astype(bf16)
    out_ref[...] = dot(pt[...], result).astype(bf16)

    for src, sem in sent:
        pltpu.make_async_copy(src, src, sem).wait()


def shards(
    residual, queries, draft_keys, draft_values, cache_keys, cache_values, tenant_ids, tree_mask,
    cache_lengths, out_weight, out_signs, norm_gain, gate_weight, up_weight, down_weight,
    gate_signs, up_signs, down_signs, delta_scale,
):
    hbm = pl.BlockSpec(memory_space=pl.ANY)
    smem = pl.BlockSpec(memory_space=pltpu.SMEM)
    vm = pltpu.VMEM
    dma = pltpu.SemaphoreType.DMA
    scratch = [
        vm((1, 64), i32), vm((64, 64), i32), vm((64, 4096), bf16), vm((64, 4096), bf16),
        vm((2, SLOTS, 512), bf16), vm((2, SLOTS, 512), bf16), vm((64, 512), bf16),
        vm((64, 512), bf16), vm((64, 64), f32), vm((64, 64), bf16), vm((64, 64), bf16),
        vm((4096, 128), bf16), vm((2, 4096, 128), bf16), vm((8192, 128), bf16),
        vm((8192, 128), bf16), vm((128, 8192), bf16), vm((2, 8192, 128), bf16),
        vm((2, 8192, 128), bf16), vm((2, 128, 8192), bf16),
        vm((2, 64, 128), bf16), vm((2, 1, 128), f32),
        vm((4, 9, 32, 128), bf16), vm((4, 9, 32, 128), bf16),
        vm((4, 9, 32, 128), bf16), vm((3, 9, 32, 128), bf16),
        vm((4, 3, 32, 128), bf16), vm((3, 3, 32, 128), bf16),
        vm((3, 32, 128), bf16), vm((3, 32, 128), bf16),
        vm((2, 4, 4, 32, 256), bf16), vm((4, 64, 128), bf16), vm((2, 64, 128), f32),
        vm((2, 4, 4, 64, 256), bf16), vm((10, 1, 128), f32),
        vm((4, 4, 64, 256), bf16), vm((4, 4, 64, 256), bf16), vm((4, 64, 256), f32),
        vm((3, 4, 64, 256), bf16), vm((3, 4, 64, 256), bf16),
        vm((3, 64, 256), bf16), vm((3, 64, 256), bf16),
        vm((2, 64, 128), bf16), vm((4, 64, 128), bf16),
        dma((19,)), dma((4,)), dma((4,)), dma((3,)), dma((3,)), dma((3,)), dma((3,)),
        dma((1,)), dma((1,)), dma((2,)), dma((2,)),
        dma((3,)), dma((3,)), dma((3, 4)), dma((3, 4)), dma((4, 4)), dma((4, 4)),
        dma((3,)), dma((3,)),
        dma((3,)), dma((3,)), dma((3, 4)), dma((3, 4)), dma((4, 4)), dma((4, 4)),
        dma((7,)), dma((7,)),
        dma((4,)), dma((4,)), dma((3,)), dma((3,)), dma((3,)), dma((3,)), dma((3,)), dma((3,)),
    ]
    return pl.pallas_call(
        layer,
        name="layer",
        out_shape=jax.ShapeDtypeStruct((64, 128), bf16),
        in_specs=[hbm, hbm, smem, smem] + [hbm] * 15,
        out_specs=pl.BlockSpec(memory_space=pltpu.VMEM),
        scratch_shapes=scratch,
        compiler_params=pltpu.CompilerParams(
            collective_id=0, has_side_effects=True, vmem_limit_bytes=60 * 1024 * 1024
        ),
    )(
        tenant_ids.reshape(1, 64), tree_mask, cache_lengths, delta_scale, residual, queries,
        draft_keys, draft_values, cache_keys, cache_values, out_weight, out_signs,
        norm_gain.reshape(1, 128), gate_weight, up_weight, down_weight, gate_signs, up_signs,
        down_signs,
    )


def solution(mesh):
    return jax.shard_map(
        shards,
        mesh=mesh,
        in_specs=(
            P(None, "ctx"),
            P(None, "kv"),
            P(None, "kv"),
            P(None, "kv"),
            P(None, "ctx", "kv"),
            P(None, "ctx", "kv"),
            P(),
            P(),
            P(),
            P("kv", "ctx"),
            P(None, "kv", "ctx"),
            P("ctx"),
            P(None, ("kv", "ctx")),
            P(None, ("kv", "ctx")),
            P(("kv", "ctx"), None),
            P(None, None, ("kv", "ctx")),
            P(None, None, ("kv", "ctx")),
            P(None, ("kv", "ctx"), None),
            P(),
        ),
        out_specs=P(None, "ctx"),
        check_vma=False,
    )
```

```python
import functools

import jax
import jax.numpy as jnp
from jax import lax
from jax.experimental import pallas as pl
from jax.experimental.pallas import tpu as pltpu
from jax.sharding import PartitionSpec as P

D = 8192
FF = 16384
HEAD = 128
SLOTS = 512
NEG = -1e30
LOG2E = 1.4426950408889634
EPS = 1e-05
MESH = pl.DeviceIdType.MESH
f32, bf16, i32 = jnp.float32, jnp.bfloat16, jnp.int32
ORDER = (2, 1, 3)
NEAR = (1, 3, 2)


def dot(a, b, dims=((1,), (0,))):
    return lax.dot_general(a, b, (dims, ((), ())), preferred_element_type=f32)


def mult(v, n):
    return pl.multiple_of(v, n)


def lanes():
    return lax.broadcasted_iota(i32, (32, 128), 1)


def split(st):
    hi = st.astype(bf16).astype(f32)
    mid = (st - hi).astype(bf16).astype(f32)
    lo = st - hi - mid
    lane = lanes()
    return jnp.where(
        lane < 32, hi, jnp.where(lane < 64, mid, jnp.where(lane < 96, lo, 0.0))
    ).astype(bf16)


def join(block):
    v = block.astype(f32)
    v = v + pltpu.roll(v, 32, 1)
    return v + pltpu.roll(v, 64, 1)


def blend(stats):
    top = functools.reduce(jnp.maximum, stats)
    parts = [jnp.exp(s - top) for s in stats]
    total = functools.reduce(jnp.add, parts)
    inverse = 1.0 / total
    return [w * inverse for w in parts], top + jnp.log(total)


def mixed_of(factors, blocks, k):
    terms = [f[:, k : k + 1] * b for f, b in zip(factors, blocks)]
    return functools.reduce(jnp.add, terms)


def layer(
    ids_h, mask_h, lens, dsc, res_h, q_h, dk_h, dv_h, ck_h, cv_h, wo_h, so_h, gain_h,
    wg_h, wu_h, wd_h, sg_h, su_h, sd_h,
    out_ref,
    ids, mask, qraw, qs, kc, vc, dk, dv, vis, pm, pt, wo, so, wg, wu, wd, sg, su, sd,
    rres, gains, acs, acr, a1s, a1r, a2s, a2r, ab, yb, hid, gb, ss,
    ecs, ecr, e1o, e1s, e1r, e2s, e2r, e3s, e3r,
    ls, c_s, c_r, a1_s, a1_r, a2_s, a2_r, r_s, r_r,
    bq_s, bq_r, bp_s, bp_r, bc_s, bc_r, y_s, y_r,
    dq_s, dq_r, dp_s, dp_r, dc_s, dc_r, n_s, n_r,
    e0_s, e0_r, e1_s, e1_r, e2_s, e2_r, e3_s, e3_r,
):
    kv, ctx = lax.axis_index("kv"), lax.axis_index("ctx")
    c = ctx % 2
    yh = (ctx // 2) % 2
    x = (ctx // 4) % 4
    z = ctx // 16
    p = z + c * (x - z)
    q = x + c * (z - x)
    sp, sq = 16 - 12 * c, 4 + 12 * c
    yi = yh * 2 + kv
    oc = 1 - c

    core = (kv, ctx + 1 - 2 * c)

    def p_dev(d):
        return (kv, ctx + ((p + d) % 4 - p) * sp)

    def q_dev(d):
        return (kv, ctx + ((q + d) % 4 - q) * sq)

    def y_dev(d):
        to = (yi + d) % 4
        return (to % 2, ctx + (to // 2 - yh) * 2)

    def qy_dev(d, e):
        return (kv, q_dev(d)[1] + e * (2 - 4 * yh))

    near_step = 3 - 2 * (yi % 2)
    near = y_dev(near_step)

    barrier = pltpu.get_barrier_semaphore()
    peers = [core] + [p_dev(d) for d in NEAR] + [q_dev(d) for d in NEAR] + [y_dev(d) for d in NEAR]
    peers += [qy_dev(d, 1) for d in NEAR]
    def load(n, src, dst):
        copy = pltpu.make_async_copy(src, dst, ls.at[n])
        copy.start()
        return copy

    first = [load(0, ids_h, ids), load(1, q_h, qraw)]
    for peer in peers:
        pl.semaphore_signal(barrier, inc=1, device_id=peer, device_id_type=MESH)
    other_keys = load(2, ck_h.at[oc], kc.at[oc])
    other_values = load(3, cv_h.at[oc], vc.at[oc])
    own_keys = load(4, ck_h.at[c], kc.at[c])
    own_values = load(5, cv_h.at[c], vc.at[c])
    small = [
        load(6, mask_h, mask), load(7, dk_h, dk), load(8, dv_h, dv),
        load(9, res_h, rres.at[yh]), load(10, gain_h, gains.at[yh]),
    ]

    sent = []

    def send(src, dst, s_sem, r_sem, to):
        copy = pltpu.make_async_remote_copy(
            src_ref=src, dst_ref=dst, send_sem=s_sem, recv_sem=r_sem,
            device_id=to, device_id_type=MESH,
        )
        copy.start()
        sent.append((src, s_sem))

    def arrived(dst, sem):
        pltpu.make_async_copy(dst, dst, sem).wait()

    for copy in first:
        copy.wait()
    row = jnp.broadcast_to(ids[...].astype(f32), (64, 64))
    ii = lax.broadcasted_iota(i32, (64, 64), 0)
    jj = lax.broadcasted_iota(i32, (64, 64), 1)
    col = jnp.sum(jnp.where(ii == jj, row, 0.0), axis=1, keepdims=True)
    same = jnp.where(row == col, 1.0, 0.0)
    pos_col = jnp.sum(jnp.where(jj < ii, same, 0.0), axis=1, keepdims=True) + 32.0 * col
    pos_row = jnp.sum(jnp.where(ii < jj, same, 0.0), axis=0, keepdims=True) + 32.0 * row[:1]
    pt[...] = jnp.where(pos_col == jj.astype(f32), 1.0, 0.0).astype(bf16)
    pm[...] = jnp.where(pos_row == ii.astype(f32), 1.0, 0.0).astype(bf16)

    @pl.loop(0, 4)
    def _(n):
        at = pl.ds(mult(n * 1024, 1024), 1024)
        qs[:, at] = dot(pm[...], qraw[:, at]).astype(bf16)

    factor = HEAD ** (-0.5)
    c32, o32 = mult(c * 32, 32), mult(oc * 32, 32)
    first_slot = ctx * SLOTS

    def attend(t, t32, g):
        rows = jnp.concatenate(
            [qs[pl.ds(t32, 32), pl.ds(mult((g * 8 + k) * 128, 128), 128)] for k in range(8)], axis=0
        )
        at = pl.ds(mult(g * 128, 128), 128)
        s = dot(rows, kc[t, :, at], ((1,), (1,)))
        live = lax.broadcasted_iota(i32, (1, SLOTS), 1) + first_slot < lens[t]
        s = jnp.where(live, s, NEG)
        m = jnp.max(s, axis=1, keepdims=True)
        m = jnp.where(m > 0.5 * NEG, m, 0.0)
        e = jnp.exp2((s - m) * (factor * LOG2E))
        l = jnp.sum(e, axis=1, keepdims=True)
        o = dot(e.astype(bf16), vc[t, :, at])
        some = l > 0.0
        safe = jnp.where(some, l, 1.0)
        o = o * (1.0 / safe)
        lse = jnp.where(some, m * factor + jnp.log(safe), NEG)
        lane = lanes() % 32
        st = jnp.zeros((32, 128), f32)
        for k in range(8):
            st = jnp.where(lane == k, lse[k * 32 : (k + 1) * 32], st)
        return o, st

    other_keys.wait()
    other_values.wait()
    rest = [
        load(11, wo_h, wo), load(12, so_h, so), load(13, wg_h, wg), load(14, wu_h, wu),
        load(15, sg_h, sg), load(16, su_h, su), load(17, wd_h, wd), load(18, sd_h, sd),
    ]
    def offset(i):
        return 2 - i + 3 * (i // 2) - 2 * (i // 3)

    def other_block(d):
        o, st = attend(oc, o32, (q + d) % 4)
        for k in range(8):
            acs[d, k] = o[k * 32 : (k + 1) * 32].astype(bf16)
        acs[d, 8] = split(st)

    def other_send(d):
        pltpu.make_async_remote_copy(
            src_ref=acs.at[d], dst_ref=acr.at[d], send_sem=c_s.at[d], recv_sem=c_r.at[d],
            device_id=core, device_id_type=MESH,
        ).start()

    other_block(2)
    pl.semaphore_wait(barrier, len(peers))
    other_send(2)

    @pl.loop(1, 4)
    def _(i):
        d = offset(i)
        other_block(d)
        other_send(d)

    own_keys.wait()
    own_values.wait()
    for copy in small:
        copy.wait()
    send(rres.at[yh], rres.at[yh], r_s.at[0], r_r.at[0], near)
    send(gains.at[yh], gains.at[yh], r_s.at[1], r_r.at[1], near)

    @pl.loop(0, 4)
    def _(i):
        d = offset(i)
        o, st = attend(c, c32, (p + d) % 4)
        arrived(acr.at[d], c_r.at[d])
        factors, lse = blend([st, join(acr[d, 8])])
        for k in range(8):
            blocks = [o[k * 32 : (k + 1) * 32], acr[d, k].astype(f32)]
            a1s[d, k] = mixed_of(factors, blocks, k).astype(bf16)
        a1s[d, 8] = split(lse)

        @pl.when(d != 0)
        def _():
            pltpu.make_async_remote_copy(
                src_ref=a1s.at[d], dst_ref=a1r.at[d - 1], send_sem=a1_s.at[d - 1],
                recv_sem=a1_r.at[d - 1], device_id=p_dev(d), device_id_type=MESH,
            ).start()

    for d in range(4):
        sent.append((acs.at[d], c_s.at[d]))
    for d in ORDER:
        sent.append((a1s.at[d], a1_s.at[d - 1]))

    vis[...] = dot(pm[...], mask[...].astype(f32).astype(bf16))
    head0 = p * 8 + q * 2
    rows = jnp.concatenate(
        [qs[pl.ds(c32, 32), pl.ds(mult((head0 + k) * 128, 128), 128)] for k in range(2)], axis=0
    )
    at_p = pl.ds(mult(p * 128, 128), 128)
    seen = jnp.concatenate([vis[pl.ds(c32, 32), :]] * 2, axis=0) > 0.5
    s = jnp.where(seen, dot(rows, dk[:, at_p], ((1,), (1,))) * factor, NEG)
    m = jnp.max(s, axis=1, keepdims=True)
    e = jnp.where(seen, jnp.exp(s - m), 0.0)
    l = jnp.sum(e, axis=1, keepdims=True)
    draft_o = dot(e.astype(bf16), dv[:, at_p]) * (1.0 / l)
    lse = m + jnp.log(l)
    draft_st = jnp.where(lanes() % 32 == 0, lse[:32], lse[32:])

    for d in NEAR:
        arrived(a1r.at[d - 1], a1_r.at[d - 1])
    sources = [a1s.at[0]] + [a1r.at[n] for n in range(3)]
    factors, lse = blend([join(s[8]) for s in sources])
    keep = None
    for d in ORDER + (0,):
        to_q = (q + d) % 4
        shift = (128 - 2 * to_q) % 128
        turned = [pltpu.roll(f, shift, 1) for f in factors]
        heads = [
            mixed_of(turned, [s[2 * to_q + k].astype(f32) for s in sources], k) for k in range(2)
        ]
        st = pltpu.roll(lse, shift, 1)
        a2s[d, 0] = heads[0].astype(bf16)
        a2s[d, 1] = heads[1].astype(bf16)
        a2s[d, 2] = split(st)
        for e in (1, 0):
            if d or e:
                send(a2s.at[d], a2r.at[e, d], a2_s.at[e, d], a2_r.at[e, d], qy_dev(d, e))
        if not d:
            keep = (heads, st)

    others = [(0, 1), (0, 3), (1, 0), (1, 1), (1, 3), (0, 2), (1, 2)]
    for e, d in others:
        arrived(a2r.at[e, d], a2_r.at[e, d])
    factors, _ = blend([keep[1]] + [join(a2r[e, d, 2]) for e, d in others] + [draft_st])
    for k in range(2):
        blocks = [keep[0][k]] + [a2r[e, d, k].astype(f32) for e, d in others]
        blocks.append(draft_o[k * 32 : (k + 1) * 32])
        ab[c, p, q, :, k * 128 : (k + 1) * 128] = mixed_of(factors, blocks, k).astype(bf16)

    def nothing():
        pass

    def gather(buf, q_s, q_r, p_s, p_r, k_s, k_r, ring, after_q=nothing, after_p=nothing):
        def unit(dp, dq):
            return buf.at[c, (p - dp + 4) % 4, (q - dq + 4) % 4]

        def theirs(dp, dq):
            return buf.at[oc, (q - dp + 4) % 4, (p - dq + 4) % 4]

        def to_core(dp, dq):
            at = unit(dp, dq)
            send(at, at, k_s.at[dp, dq], k_r.at[dp, dq], core)

        def to_p(dq):
            at = unit(0, dq)
            for d in ORDER:
                send(at, at, p_s.at[d - 1, dq], p_r.at[d - 1, dq], p_dev(d))

        at = unit(0, 0)
        for d in ORDER:
            send(at, at, q_s.at[d - 1], q_r.at[d - 1], q_dev(d))
        to_p(0)
        to_core(0, 0)
        for dq in NEAR:
            arrived(unit(0, dq), q_r.at[dq - 1])
            to_p(dq)
            to_core(0, dq)
        after_q()

        def own_batch(dp):
            if dp:
                for dq in (0,) + NEAR:
                    arrived(unit(dp, dq), p_r.at[dp - 1, dq])
                    to_core(dp, dq)
            ring(c, (p - dp + 4) % 4, True)

        def core_batch(dp):
            for dq in (0,) + NEAR:
                arrived(theirs(dp, dq), k_r.at[dp, dq])
            ring(oc, (q - dp + 4) % 4, False)

        own_batch(0)
        own_batch(1)
        core_batch(0)
        own_batch(3)
        core_batch(1)
        own_batch(2)
        after_p()
        core_batch(3)
        core_batch(2)

    rest[0].wait()
    rest[1].wait()
    partial = {True: None, False: None}

    def out_batch(t, at_p, mine):
        lhs = jnp.concatenate([ab[t, at_p, n] for n in range(4)], axis=1)
        at = pl.ds(mult(at_p * 1024, 1024), 1024)
        both = jnp.concatenate([wo[at, :], so[t, at, :]], axis=1)
        value = dot(lhs, both)
        partial[mine] = value if partial[mine] is None else partial[mine] + value

    gather(ab, bq_s, bq_r, bp_s, bp_r, bc_s, bc_r, out_batch)
    for mine, t, t32 in ((True, c, c32), (False, oc, o32)):
        value = partial[mine]
        value = value[:, :128] + (dsc[t, 0] * D ** (-0.5)) * value[:, 128:]
        yb[yi, pl.ds(t32, 32), :] = value.astype(bf16)

    for d in ORDER:
        send(yb.at[yi], yb.at[yi], y_s.at[d - 1], y_r.at[d - 1], y_dev(d))
    arrived(rres.at[1 - yh], r_r.at[0])
    arrived(gains.at[1 - yh], r_r.at[1])
    base = [dot(pm[...], rres[b]) for b in range(2)]
    for d in NEAR:
        arrived(yb.at[(yi - d + 4) % 4], y_r.at[d - 1])
    squares = jnp.zeros((64, 1), f32)
    for b in range(2):
        h = base[b] + (yb[2 * b].astype(f32) + yb[2 * b + 1].astype(f32))
        hid[b] = h
        gb[c, p, q, :, b * 128 : (b + 1) * 128] = (h * gains[b]).astype(bf16)
        squares = squares + jnp.sum(h * h, axis=1, keepdims=True)
    ss[0, :, 0:64] = jnp.sum(jnp.where(ii == jj, squares, 0.0), axis=0, keepdims=True)
    ss[0, :, 64:128] = jnp.zeros((1, 64), f32)
    for d in ORDER:
        send(ss.at[0], ss.at[d], n_s.at[d - 1], n_r.at[d - 1], q_dev(d))

    for n in range(2, 6):
        rest[n].wait()
    sums = [None, None, None]

    def up_batch(t, at_p, mine):
        tp, tq = (sp, sq) if mine else (sq, sp)
        lhs = jnp.concatenate([gb[t, at_p, n] for n in range(4)], axis=1)

        def rows(ref, *lead):
            parts = []
            for n in range(4):
                start = (at_p * tp + n * tq + t) * 128
                for b in range(2):
                    parts.append(ref[(*lead, pl.ds(mult(start + b * 256, 128), 128), slice(None))])
            return jnp.concatenate(parts, axis=0)

        values = [dot(lhs, jnp.concatenate([rows(wg), rows(wu)], axis=1))]
        for n in range(2):
            both = jnp.concatenate([rows(sg, n), rows(su, n)], axis=1)
            values.append(dot(lhs[n * 32 : (n + 1) * 32], both))
        for n in range(3):
            sums[n] = values[n] if sums[n] is None else sums[n] + values[n]

    def squares_q():
        for d in NEAR:
            arrived(ss.at[d], n_r.at[d - 1])
        ss[4] = ss[0] + ss[1] + ss[2] + ss[3]
        for d in ORDER:
            send(ss.at[4], ss.at[4 + d], n_s.at[2 + d], n_r.at[2 + d], p_dev(d))

    def squares_p():
        for d in NEAR:
            arrived(ss.at[4 + d], n_r.at[2 + d])
        ss[8] = ss[4] + ss[5] + ss[6] + ss[7]
        send(ss.at[8], ss.at[9], n_s.at[6], n_r.at[6], core)

    gather(gb, dq_s, dq_r, dp_s, dp_r, dc_s, dc_r, up_batch, squares_q, squares_p)
    arrived(ss.at[9], n_r.at[6])
    whole = (ss[8] + ss[9])[:, 0:64]
    total = jnp.sum(jnp.where(ii == jj, whole, 0.0), axis=1, keepdims=True)
    scale = lax.rsqrt(total * (1.0 / D) + EPS)

    def halves(n, at):
        return dsc[0, n] * at, dsc[1, n] * at

    g0, g1 = halves(1, D ** (-0.5))
    u0, u1 = halves(2, D ** (-0.5))
    gate_delta = jnp.concatenate([g0 * sums[1][:, :128], g1 * sums[2][:, :128]], axis=0)
    up_delta = jnp.concatenate([u0 * sums[1][:, 128:], u1 * sums[2][:, 128:]], axis=0)
    gate = (sums[0][:, :128] + gate_delta) * scale
    up = (sums[0][:, 128:] + up_delta) * scale
    active = (gate / (1.0 + jnp.exp(-gate)) * up).astype(bf16)

    rest[6].wait()
    rest[7].wait()
    d0, d1 = halves(3, FF ** (-0.5))

    def down(t, at_p, tp, n, tq):
        start = (at_p * tp + n * tq + t) * 128

        def cols(ref, *lead):
            return jnp.concatenate(
                [
                    ref[(*lead, slice(None), pl.ds(mult(start + b * 256, 128), 128))]
                    for b in range(2)
                ],
                axis=1,
            )

        value = dot(active, cols(wd))
        delta = [d0 * dot(active[:32], cols(sd, 0)), d1 * dot(active[32:], cols(sd, 1))]
        return value + jnp.concatenate(delta, axis=0)

    def down_other(d):
        for n in range(4):
            ecs[d, n] = down(oc, (q + d) % 4, sq, n, sp).astype(bf16)
        send(ecs.at[d], ecr.at[d], e0_s.at[d], e0_r.at[d], core)

    def down_own(d):
        mine = [down(c, (p + d) % 4, sp, n, sq) for n in range(4)]
        arrived(ecr.at[d], e0_r.at[d])
        for n in range(4):
            value = mine[n] + ecr[d, n].astype(f32)
            if d:
                e1s[d - 1, n] = value.astype(bf16)
            else:
                e1o[n] = value
        if d:
            send(e1s.at[d - 1], e1r.at[d - 1], e1_s.at[d - 1], e1_r.at[d - 1], p_dev(d))

    down_other(2)
    down_other(1)
    down_other(3)
    down_own(2)
    down_other(0)
    down_own(1)
    down_own(3)
    down_own(0)
    for d in NEAR:
        arrived(e1r.at[d - 1], e1_r.at[d - 1])
    kept = None
    for d in ORDER + (0,):
        n = (q + d) % 4
        value = e1o[n]
        for s in range(3):
            value = value + e1r[s, n].astype(f32)
        if d:
            e2s[d - 1] = value.astype(bf16)
            send(e2s.at[d - 1], e2r.at[d - 1], e2_s.at[d - 1], e2_r.at[d - 1], q_dev(d))
        else:
            kept = value
    for d in NEAR:
        arrived(e2r.at[d - 1], e2_r.at[d - 1])
        kept = kept + e2r[d - 1].astype(f32)
    for b in range(2):
        e3s[b] = kept[:, b * 128 : (b + 1) * 128].astype(bf16)
    for d in ORDER:
        to_block = ((yi + d) % 4) // 2
        send(e3s.at[to_block], e3r.at[yi], e3_s.at[d - 1], e3_r.at[d - 1], y_dev(d))
    e3r[yi] = e3s[yh]
    for d in NEAR:
        arrived(e3r.at[(yi - d + 4) % 4], e3_r.at[d - 1])
    lowered = (e3r[0].astype(f32) + e3r[1].astype(f32)) + (e3r[2].astype(f32) + e3r[3].astype(f32))
    result = (hid[yh] + lowered).astype(bf16)
    out_ref[...] = dot(pt[...], result).astype(bf16)

    for src, sem in sent:
        pltpu.make_async_copy(src, src, sem).wait()


def shards(
    residual, queries, draft_keys, draft_values, cache_keys, cache_values, tenant_ids, tree_mask,
    cache_lengths, out_weight, out_signs, norm_gain, gate_weight, up_weight, down_weight,
    gate_signs, up_signs, down_signs, delta_scale,
):
    hbm = pl.BlockSpec(memory_space=pltpu.HBM)
    smem = pl.BlockSpec(memory_space=pltpu.SMEM)
    vm = pltpu.VMEM
    dma = pltpu.SemaphoreType.DMA
    scratch = [
        vm((1, 64), i32), vm((64, 64), i32), vm((64, 4096), bf16), vm((64, 4096), bf16),
        vm((2, SLOTS, 512), bf16), vm((2, SLOTS, 512), bf16), vm((64, 512), bf16),
        vm((64, 512), bf16), vm((64, 64), f32), vm((64, 64), bf16), vm((64, 64), bf16),
        vm((4096, 128), bf16), vm((2, 4096, 128), bf16), vm((8192, 128), bf16),
        vm((8192, 128), bf16), vm((128, 8192), bf16), vm((2, 8192, 128), bf16),
        vm((2, 8192, 128), bf16), vm((2, 128, 8192), bf16),
        vm((2, 64, 128), bf16), vm((2, 1, 128), f32),
        vm((4, 9, 32, 128), bf16), vm((4, 9, 32, 128), bf16),
        vm((4, 9, 32, 128), bf16), vm((3, 9, 32, 128), bf16),
        vm((4, 3, 32, 128), bf16), vm((2, 4, 3, 32, 128), bf16),
        vm((2, 4, 4, 32, 256), bf16), vm((4, 64, 128), bf16), vm((2, 64, 128), f32),
        vm((2, 4, 4, 64, 256), bf16), vm((10, 1, 128), f32),
        vm((4, 4, 64, 256), bf16), vm((4, 4, 64, 256), bf16), vm((4, 64, 256), f32),
        vm((3, 4, 64, 256), bf16), vm((3, 4, 64, 256), bf16),
        vm((3, 64, 256), bf16), vm((3, 64, 256), bf16),
        vm((2, 64, 128), bf16), vm((4, 64, 128), bf16),
        dma((19,)), dma((4,)), dma((4,)), dma((3,)), dma((3,)), dma((2, 4)), dma((2, 4)),
        dma((2,)), dma((2,)),
        dma((3,)), dma((3,)), dma((3, 4)), dma((3, 4)), dma((4, 4)), dma((4, 4)),
        dma((3,)), dma((3,)),
        dma((3,)), dma((3,)), dma((3, 4)), dma((3, 4)), dma((4, 4)), dma((4, 4)),
        dma((7,)), dma((7,)),
        dma((4,)), dma((4,)), dma((3,)), dma((3,)), dma((3,)), dma((3,)), dma((3,)), dma((3,)),
    ]
    return pl.pallas_call(
        layer,
        name="layer",
        out_shape=pltpu.VMEM((64, 128), bf16),
        in_specs=[hbm, hbm, smem, smem] + [hbm] * 15,
        out_specs=pl.BlockSpec(memory_space=pltpu.VMEM),
        scratch_shapes=scratch,
        compiler_params=pltpu.CompilerParams(
            collective_id=0, has_side_effects=True, vmem_limit_bytes=60 * 1024 * 1024
        ),
    )(
        tenant_ids.reshape(1, 64), tree_mask, cache_lengths, delta_scale, residual, queries,
        draft_keys, draft_values, cache_keys, cache_values, out_weight, out_signs,
        norm_gain.reshape(1, 128), gate_weight, up_weight, down_weight, gate_signs, up_signs,
        down_signs,
    )


def solution(mesh):
    return jax.shard_map(
        shards,
        mesh=mesh,
        in_specs=(
            P(None, "ctx"),
            P(None, "kv"),
            P(None, "kv"),
            P(None, "kv"),
            P(None, "ctx", "kv"),
            P(None, "ctx", "kv"),
            P(),
            P(),
            P(),
            P("kv", "ctx"),
            P(None, "kv", "ctx"),
            P("ctx"),
            P(None, ("kv", "ctx")),
            P(None, ("kv", "ctx")),
            P(("kv", "ctx"), None),
            P(None, None, ("kv", "ctx")),
            P(None, None, ("kv", "ctx")),
            P(None, ("kv", "ctx"), None),
            P(),
        ),
        out_specs=P(None, "ctx"),
        check_vma=False,
    )
```

```python
import functools

import jax
import jax.numpy as jnp
from jax import lax
from jax.experimental import pallas as pl
from jax.experimental.pallas import tpu as pltpu
from jax.sharding import PartitionSpec as P

D = 8192
FF = 16384
HEAD = 128
SLOTS = 512
NEG = -1e30
LOG2E = 1.4426950408889634
EPS = 1e-05
MESH = pl.DeviceIdType.MESH
f32, bf16, i32 = jnp.float32, jnp.bfloat16, jnp.int32
ORDER = (2, 1, 3)
NEAR = (1, 3, 2)


def dot(a, b, dims=((1,), (0,))):
    return lax.dot_general(a, b, (dims, ((), ())), preferred_element_type=f32)


def mult(v, n):
    return pl.multiple_of(v, n)


def lanes():
    return lax.broadcasted_iota(i32, (32, 128), 1)


def split(st):
    hi = st.astype(bf16).astype(f32)
    mid = (st - hi).astype(bf16).astype(f32)
    lo = st - hi - mid
    lane = lanes()
    return jnp.where(
        lane < 32, hi, jnp.where(lane < 64, mid, jnp.where(lane < 96, lo, 0.0))
    ).astype(bf16)


def join(block):
    v = block.astype(f32)
    v = v + pltpu.roll(v, 32, 1)
    return v + pltpu.roll(v, 64, 1)


def blend(stats):
    top = functools.reduce(jnp.maximum, stats)
    parts = [jnp.exp(s - top) for s in stats]
    total = functools.reduce(jnp.add, parts)
    inverse = 1.0 / total
    return [w * inverse for w in parts], top + jnp.log(total)


def mixed_of(factors, blocks, k):
    terms = [f[:, k : k + 1] * b for f, b in zip(factors, blocks)]
    return functools.reduce(jnp.add, terms)


def layer(
    ids_h, mask_h, lens_h, dsc_h, res_h, q_h, dk_h, dv_h, ck_h, cv_h, wo_h, so_h, gain_h,
    wg_h, wu_h, wd_h, sg_h, su_h, sd_h,
    out_ref,
    lens, dsc, ids, mask, qraw, qs, kc, vc, dk, dv, vis, pm, pt, wo, so, wg, wu, wd, sg, su, sd,
    rres, gains, acs, acr, a1s, a1r, a2s, a2r, ab, yb, hid, gb, ss,
    ecs, ecr, e1o, e1s, e1r, e3s, e3r,
    ls, sem_s, c_r, a1_r, a2_r, r_r, bq_r, bp_r, bc_r, y_r, dq_r, dp_r, dc_r, n_r, e0_r, e1_r, e3_r,
):
    kv, ctx = lax.axis_index("kv"), lax.axis_index("ctx")
    c = ctx % 2
    yh = (ctx // 2) % 2
    x = (ctx // 4) % 4
    z = ctx // 16
    p = z + c * (x - z)
    q = x + c * (z - x)
    sp, sq = 16 - 12 * c, 4 + 12 * c
    yi = yh * 2 + kv
    oc = 1 - c

    core = (kv, ctx + 1 - 2 * c)

    def p_dev(d):
        return (kv, ctx + ((p + d) % 4 - p) * sp)

    def q_dev(d):
        return (kv, ctx + ((q + d) % 4 - q) * sq)

    def y_dev(d):
        to = (yi + d) % 4
        return (to % 2, ctx + (to // 2 - yh) * 2)

    def pq_dev(d, e):
        return (kv, p_dev(d)[1] + q_dev(e)[1] - ctx)

    def qy_dev(d, e):
        return (kv, q_dev(d)[1] + e * (2 - 4 * yh))

    near_step = 3 - 2 * (yi % 2)
    near = y_dev(near_step)

    barrier = pltpu.get_barrier_semaphore()
    peers = [core] + [p_dev(d) for d in NEAR] + [q_dev(d) for d in NEAR] + [y_dev(d) for d in NEAR]
    peers += [qy_dev(d, 1) for d in NEAR]
    peers += [pq_dev(d, e) for d in NEAR for e in NEAR]
    def load(n, src, dst):
        copy = pltpu.make_async_copy(src, dst, ls.at[n])
        copy.start()
        return copy

    first = [load(0, ids_h, ids), load(1, q_h, qraw), load(17, lens_h, lens), load(18, dsc_h, dsc)]
    for peer in peers:
        pl.semaphore_signal(barrier, inc=1, device_id=peer, device_id_type=MESH)
    load(2, ck_h.at[oc], kc.at[oc])
    load(2, cv_h.at[oc], vc.at[oc])
    load(3, ck_h.at[c], kc.at[c])
    load(3, cv_h.at[c], vc.at[c])
    small = [
        load(4, mask_h, mask), load(5, dk_h, dk), load(6, dv_h, dv),
        load(7, res_h, rres.at[yh]), load(8, gain_h, gains.at[yh]),
    ]

    big, tiny = [0], [0]

    def send(src, dst, r_sem, to):
        size = 1
        for n in src.shape:
            size *= n
        small_one = src.dtype == f32
        (tiny if small_one else big)[0] += size * (4 if small_one else 2)
        pltpu.make_async_remote_copy(
            src_ref=src, dst_ref=dst, send_sem=sem_s.at[1 if small_one else 0], recv_sem=r_sem,
            device_id=to, device_id_type=MESH,
        ).start()

    def arrived(dst, sem):
        pltpu.make_async_copy(dst, dst, sem).wait()

    for copy in first:
        copy.wait()
    row = jnp.broadcast_to(ids[...].astype(f32), (64, 64))
    ii = lax.broadcasted_iota(i32, (64, 64), 0)
    jj = lax.broadcasted_iota(i32, (64, 64), 1)
    col = jnp.sum(jnp.where(ii == jj, row, 0.0), axis=1, keepdims=True)
    same = jnp.where(row == col, 1.0, 0.0)
    pos_col = jnp.sum(jnp.where(jj < ii, same, 0.0), axis=1, keepdims=True) + 32.0 * col
    pos_row = jnp.sum(jnp.where(ii < jj, same, 0.0), axis=0, keepdims=True) + 32.0 * row[:1]
    pt[...] = jnp.where(pos_col == jj.astype(f32), 1.0, 0.0).astype(bf16)
    pm[...] = jnp.where(pos_row == ii.astype(f32), 1.0, 0.0).astype(bf16)

    for n in range(4):
        at = pl.ds(n * 1024, 1024)
        qs[:, at] = dot(pm[...], qraw[:, at]).astype(bf16)

    factor = HEAD ** (-0.5)
    c32, o32 = mult(c * 32, 32), mult(oc * 32, 32)
    first_slot = ctx * SLOTS

    def attend(t, t32, g):
        rows = jnp.concatenate(
            [qs[pl.ds(t32, 32), pl.ds(mult((g * 8 + k) * 128, 128), 128)] for k in range(8)], axis=0
        )
        at = pl.ds(mult(g * 128, 128), 128)
        s = dot(rows, kc[t, :, at], ((1,), (1,)))
        live = lax.broadcasted_iota(i32, (1, SLOTS), 1) + first_slot < lens[t]
        s = jnp.where(live, s, NEG)
        m = jnp.max(s, axis=1, keepdims=True)
        m = jnp.where(m > 0.5 * NEG, m, 0.0)
        e = jnp.exp2((s - m) * (factor * LOG2E))
        l = jnp.sum(e, axis=1, keepdims=True)
        o = dot(e.astype(bf16), vc[t, :, at])
        some = l > 0.0
        safe = jnp.where(some, l, 1.0)
        o = o * (1.0 / safe)
        lse = jnp.where(some, m * factor + jnp.log(safe), NEG)
        lane = lanes() % 32
        st = jnp.zeros((32, 128), f32)
        for k in range(8):
            st = jnp.where(lane == k, lse[k * 32 : (k + 1) * 32], st)
        return o, st

    arrived(kc, ls.at[2])
    rest = [
        load(9, wo_h, wo), load(10, so_h, so), load(11, wg_h, wg), load(12, wu_h, wu),
        load(13, sg_h, sg), load(14, su_h, su), load(15, wd_h, wd), load(16, sd_h, sd),
    ]
    def other_block(d):
        o, st = attend(oc, o32, (q + d) % 4)
        for k in range(8):
            acs[d, k] = o[k * 32 : (k + 1) * 32].astype(bf16)
        acs[d, 8] = split(st)

    def other_send(d):
        send(acs.at[d], acr.at[d], c_r.at[d], core)

    for d in ORDER + (0,):
        other_block(d)
    pl.semaphore_wait(barrier, len(peers))
    for d in ORDER + (0,):
        other_send(d)

    arrived(kc, ls.at[3])
    for copy in small:
        copy.wait()
    send(rres.at[yh], rres.at[yh], r_r.at[0], near)
    send(gains.at[yh], gains.at[yh], r_r.at[1], near)

    def merge(d, o, st):
        factors, lse = blend([st, join(acr[d, 8])])
        for k in range(8):
            blocks = [o[k * 32 : (k + 1) * 32], acr[d, k].astype(f32)]
            a1s[d, k] = mixed_of(factors, blocks, k).astype(bf16)
        a1s[d, 8] = split(lse)
        if d:
            send(a1s.at[d], a1r.at[d - 1], a1_r.at[0], p_dev(d))

    pending = []
    for d in ORDER + (0,):
        pending.append((d, *attend(c, c32, (p + d) % 4)))
        if len(pending) > 1:
            arrived(acr.at[pending[0][0]], c_r.at[pending[0][0]])
            merge(*pending.pop(0))
    arrived(acr.at[0], c_r.at[0])
    merge(*pending.pop(0))

    vis[...] = dot(pm[...], mask[...].astype(f32).astype(bf16))
    head0 = p * 8 + q * 2
    rows = jnp.concatenate(
        [qs[pl.ds(c32, 32), pl.ds(mult((head0 + k) * 128, 128), 128)] for k in range(2)], axis=0
    )
    at_p = pl.ds(mult(p * 128, 128), 128)
    seen = jnp.concatenate([vis[pl.ds(c32, 32), :]] * 2, axis=0) > 0.5
    s = jnp.where(seen, dot(rows, dk[:, at_p], ((1,), (1,))) * factor, NEG)
    m = jnp.max(s, axis=1, keepdims=True)
    e = jnp.where(seen, jnp.exp(s - m), 0.0)
    l = jnp.sum(e, axis=1, keepdims=True)
    draft_o = dot(e.astype(bf16), dv[:, at_p]) * (1.0 / l)
    lse = m + jnp.log(l)
    draft_st = jnp.where(lanes() % 32 == 0, lse[:32], lse[32:])

    arrived(a1r, a1_r.at[0])
    sources = [a1s.at[0]] + [a1r.at[n] for n in range(3)]
    factors, lse = blend([join(s[8]) for s in sources])
    keep = None
    for d in ORDER + (0,):
        to_q = (q + d) % 4
        shift = (128 - 2 * to_q) % 128
        turned = [pltpu.roll(f, shift, 1) for f in factors]
        heads = [
            mixed_of(turned, [s[2 * to_q + k].astype(f32) for s in sources], k) for k in range(2)
        ]
        st = pltpu.roll(lse, shift, 1)
        a2s[d, 0] = heads[0].astype(bf16)
        a2s[d, 1] = heads[1].astype(bf16)
        a2s[d, 2] = split(st)
        for e in (1, 0):
            if d or e:
                send(a2s.at[d], a2r.at[4 * e + d], a2_r.at[0], qy_dev(d, e))
        if not d:
            keep = (heads, st)

    others = [(0, 1), (0, 3), (1, 0), (1, 1), (1, 3), (0, 2), (1, 2)]
    arrived(a2r.at[pl.ds(1, 7)], a2_r.at[0])
    factors, _ = blend([keep[1]] + [join(a2r[4 * e + d, 2]) for e, d in others] + [draft_st])
    for k in range(2):
        blocks = [keep[0][k]] + [a2r[4 * e + d, k].astype(f32) for e, d in others]
        blocks.append(draft_o[k * 32 : (k + 1) * 32])
        ab[c, p, q, :, k * 128 : (k + 1) * 128] = mixed_of(factors, blocks, k).astype(bf16)

    def nothing():
        pass

    def gather(buf, direct, q_r, p_r, k_r, ring, after_q=nothing, after_p=nothing):
        mine = buf.at[c, p, q]

        def row_of(dp):
            return buf.at[c, (p - dp + 4) % 4]

        def to_core(dp):
            send(row_of(dp), row_of(dp), k_r.at[dp], core)

        if direct:
            for dp in (0,) + ORDER:
                for dq in ORDER + (0,):
                    if dp or dq:
                        send(mine, mine, p_r.at[dp], pq_dev(dp, dq))
            arrived(buf.at[c, p, pl.ds(0, 3)], p_r.at[0])
        else:
            for d in ORDER:
                send(mine, mine, q_r.at[d - 1], q_dev(d))
            for d in ORDER:
                send(mine, mine, p_r.at[d], p_dev(d))
            for dq in NEAR:
                at = buf.at[c, p, (q - dq + 4) % 4]
                arrived(at, q_r.at[dq - 1])
                for d in ORDER:
                    send(at, at, p_r.at[d], p_dev(d))
        to_core(0)
        after_q()

        def own_batch(dp):
            if dp:
                arrived(row_of(dp), p_r.at[dp])
                to_core(dp)
            ring(c, (p - dp + 4) % 4, True)

        def core_batch(dp):
            at_p = (q - dp + 4) % 4
            arrived(buf.at[oc, at_p], k_r.at[dp])
            ring(oc, at_p, False)

        own_batch(0)
        own_batch(1)
        own_batch(3)
        core_batch(0)
        own_batch(2)
        after_p()
        core_batch(1)
        core_batch(3)
        core_batch(2)

    rest[0].wait()
    rest[1].wait()
    partial = {True: None, False: None}

    def out_batch(t, at_p, mine):
        lhs = jnp.concatenate([ab[t, at_p, n] for n in range(4)], axis=1)
        at = pl.ds(mult(at_p * 1024, 1024), 1024)
        both = jnp.concatenate([wo[at, :], so[t, at, :]], axis=1)
        value = dot(lhs, both)
        partial[mine] = value if partial[mine] is None else partial[mine] + value

    gather(ab, True, bq_r, bp_r, bc_r, out_batch)
    for mine, t, t32 in ((True, c, c32), (False, oc, o32)):
        value = partial[mine]
        value = value[:, :128] + (dsc[t, 0] * D ** (-0.5)) * value[:, 128:]
        yb[yi, pl.ds(t32, 32), :] = value.astype(bf16)

    for d in ORDER:
        send(yb.at[yi], yb.at[yi], y_r.at[0], y_dev(d))
    arrived(rres.at[1 - yh], r_r.at[0])
    arrived(gains.at[1 - yh], r_r.at[1])
    base = [dot(pm[...], rres[b]) for b in range(2)]
    arrived(yb.at[pl.ds(0, 3)], y_r.at[0])
    squares = jnp.zeros((64, 1), f32)
    for b in range(2):
        h = base[b] + (yb[2 * b].astype(f32) + yb[2 * b + 1].astype(f32))
        hid[b] = h
        gb[c, p, q, :, b * 128 : (b + 1) * 128] = (h * gains[b]).astype(bf16)
        squares = squares + jnp.sum(h * h, axis=1, keepdims=True)
    ss[0, :, 0:64] = jnp.sum(jnp.where(ii == jj, squares, 0.0), axis=0, keepdims=True)
    ss[0, :, 64:128] = jnp.zeros((1, 64), f32)
    for d in ORDER:
        send(ss.at[0], ss.at[d], n_r.at[0], q_dev(d))

    for n in range(2, 6):
        rest[n].wait()
    sums = [None, None, None]

    def up_batch(t, at_p, mine):
        tp, tq = (sp, sq) if mine else (sq, sp)
        lhs = jnp.concatenate([gb[t, at_p, n] for n in range(4)], axis=1)

        def rows(ref, *lead):
            parts = []
            for n in range(4):
                start = (at_p * tp + n * tq + t) * 128
                for b in range(2):
                    parts.append(ref[(*lead, pl.ds(mult(start + b * 256, 128), 128), slice(None))])
            return jnp.concatenate(parts, axis=0)

        values = [dot(lhs, jnp.concatenate([rows(wg), rows(wu)], axis=1))]
        for n in range(2):
            both = jnp.concatenate([rows(sg, n), rows(su, n)], axis=1)
            values.append(dot(lhs[n * 32 : (n + 1) * 32], both))
        for n in range(3):
            sums[n] = values[n] if sums[n] is None else sums[n] + values[n]

    def squares_q():
        arrived(ss.at[pl.ds(1, 3)], n_r.at[0])
        ss[4] = ss[0] + ss[1] + ss[2] + ss[3]
        for d in ORDER:
            send(ss.at[4], ss.at[4 + d], n_r.at[1], p_dev(d))

    def squares_p():
        arrived(ss.at[pl.ds(5, 3)], n_r.at[1])
        ss[8] = ss[4] + ss[5] + ss[6] + ss[7]
        send(ss.at[8], ss.at[9], n_r.at[2], core)

    gather(gb, True, dq_r, dp_r, dc_r, up_batch, squares_q, squares_p)
    arrived(ss.at[9], n_r.at[2])
    whole = (ss[8] + ss[9])[:, 0:64]
    total = jnp.sum(jnp.where(ii == jj, whole, 0.0), axis=1, keepdims=True)
    scale = lax.rsqrt(total * (1.0 / D) + EPS)

    def halves(n, at):
        return dsc[0, n] * at, dsc[1, n] * at

    g0, g1 = halves(1, D ** (-0.5))
    u0, u1 = halves(2, D ** (-0.5))
    gate_delta = jnp.concatenate([g0 * sums[1][:, :128], g1 * sums[2][:, :128]], axis=0)
    up_delta = jnp.concatenate([u0 * sums[1][:, 128:], u1 * sums[2][:, 128:]], axis=0)
    gate = (sums[0][:, :128] + gate_delta) * scale
    up = (sums[0][:, 128:] + up_delta) * scale
    active = (gate / (1.0 + jnp.exp(-gate)) * up).astype(bf16)

    rest[6].wait()
    rest[7].wait()
    d0, d1 = halves(3, FF ** (-0.5))

    def down(t, at_p, tp, n, tq):
        start = (at_p * tp + n * tq + t) * 128

        def cols(ref, *lead):
            return jnp.concatenate(
                [
                    ref[(*lead, slice(None), pl.ds(mult(start + b * 256, 128), 128))]
                    for b in range(2)
                ],
                axis=1,
            )

        value = dot(active, cols(wd))
        delta = [d0 * dot(active[:32], cols(sd, 0)), d1 * dot(active[32:], cols(sd, 1))]
        return value + jnp.concatenate(delta, axis=0)

    def down_other(d):
        for n in range(4):
            ecs[d, n] = down(oc, (q + d) % 4, sq, n, sp).astype(bf16)
        send(ecs.at[d], ecr.at[d], e0_r.at[d], core)

    def down_own(d):
        places = [(q + dq) % 4 for dq in ORDER + (0,)]
        mine = [down(c, (p + d) % 4, sp, n, sq) for n in places]
        arrived(ecr.at[d], e0_r.at[d])
        for dq, n, value in zip(ORDER + (0,), places, mine):
            value = value + ecr[d, n].astype(f32)
            if d or dq:
                e1s[d, dq] = value.astype(bf16)
                send(e1s.at[d, dq], e1r.at[4 * d + dq], e1_r.at[0], pq_dev(d, dq))
            else:
                e1o[...] = value

    down_other(2)
    down_other(1)
    down_other(3)
    down_own(2)
    down_other(0)
    down_own(1)
    down_own(3)
    down_own(0)
    arrived(e1r.at[pl.ds(1, 15)], e1_r.at[0])
    kept = e1o[...]
    for n in range(1, 16):
        kept = kept + e1r[n].astype(f32)
    for b in range(2):
        e3s[b] = kept[:, b * 128 : (b + 1) * 128].astype(bf16)
    for d in ORDER:
        to_block = ((yi + d) % 4) // 2
        send(e3s.at[to_block], e3r.at[yi], e3_r.at[0], y_dev(d))
    e3r[yi] = e3s[yh]
    arrived(e3r.at[pl.ds(0, 3)], e3_r.at[0])
    lowered = (e3r[0].astype(f32) + e3r[1].astype(f32)) + (e3r[2].astype(f32) + e3r[3].astype(f32))
    result = (hid[yh] + lowered).astype(bf16)
    out_ref[...] = dot(pt[...], result).astype(bf16)

    arrived(ss.at[pl.ds(0, tiny[0] // 512)], sem_s.at[1])
    arrived(sg.at[:, pl.ds(0, big[0] // 512)], sem_s.at[0])


def shards(
    residual, queries, draft_keys, draft_values, cache_keys, cache_values, tenant_ids, tree_mask,
    cache_lengths, out_weight, out_signs, norm_gain, gate_weight, up_weight, down_weight,
    gate_signs, up_signs, down_signs, delta_scale,
):
    hbm = pl.BlockSpec(memory_space=pltpu.HBM)
    vm = pltpu.VMEM
    dma = pltpu.SemaphoreType.DMA
    scratch = [
        pltpu.SMEM((2,), i32), pltpu.SMEM((2, 4), f32),
        vm((1, 64), i32), vm((64, 64), i32), vm((64, 4096), bf16), vm((64, 4096), bf16),
        vm((2, SLOTS, 512), bf16), vm((2, SLOTS, 512), bf16), vm((64, 512), bf16),
        vm((64, 512), bf16), vm((64, 64), f32), vm((64, 64), bf16), vm((64, 64), bf16),
        vm((4096, 128), bf16), vm((2, 4096, 128), bf16), vm((8192, 128), bf16),
        vm((8192, 128), bf16), vm((128, 8192), bf16), vm((2, 8192, 128), bf16),
        vm((2, 8192, 128), bf16), vm((2, 128, 8192), bf16),
        vm((2, 64, 128), bf16), vm((2, 1, 128), f32),
        vm((4, 9, 32, 128), bf16), vm((4, 9, 32, 128), bf16),
        vm((4, 9, 32, 128), bf16), vm((3, 9, 32, 128), bf16),
        vm((4, 3, 32, 128), bf16), vm((8, 3, 32, 128), bf16),
        vm((2, 4, 4, 32, 256), bf16), vm((4, 64, 128), bf16), vm((2, 64, 128), f32),
        vm((2, 4, 4, 64, 256), bf16), vm((10, 1, 128), f32),
        vm((4, 4, 64, 256), bf16), vm((4, 4, 64, 256), bf16), vm((64, 256), f32),
        vm((4, 4, 64, 256), bf16), vm((16, 64, 256), bf16),
        vm((2, 64, 128), bf16), vm((4, 64, 128), bf16),
        dma((19,)), dma((2,)), dma((4,)), dma((1,)), dma((1,)), dma((2,)),
        dma((3,)), dma((4,)), dma((4,)), dma((1,)), dma((3,)), dma((4,)), dma((4,)), dma((3,)),
        dma((4,)), dma((1,)), dma((1,)),
    ]
    return pl.pallas_call(
        layer,
        name="layer",
        out_shape=pltpu.VMEM((64, 128), bf16),
        in_specs=[hbm] * 19,
        out_specs=pl.BlockSpec(memory_space=pltpu.VMEM),
        scratch_shapes=scratch,
        compiler_params=pltpu.CompilerParams(
            collective_id=0, has_side_effects=True, vmem_limit_bytes=60 * 1024 * 1024
        ),
    )(
        tenant_ids.reshape(1, 64), tree_mask, cache_lengths, delta_scale, residual, queries,
        draft_keys, draft_values, cache_keys, cache_values, out_weight, out_signs,
        norm_gain.reshape(1, 128), gate_weight, up_weight, down_weight, gate_signs, up_signs,
        down_signs,
    )


def solution(mesh):
    return jax.shard_map(
        shards,
        mesh=mesh,
        in_specs=(
            P(None, "ctx"),
            P(None, "kv"),
            P(None, "kv"),
            P(None, "kv"),
            P(None, "ctx", "kv"),
            P(None, "ctx", "kv"),
            P(),
            P(),
            P(),
            P("kv", "ctx"),
            P(None, "kv", "ctx"),
            P("ctx"),
            P(None, ("kv", "ctx")),
            P(None, ("kv", "ctx")),
            P(("kv", "ctx"), None),
            P(None, None, ("kv", "ctx")),
            P(None, None, ("kv", "ctx")),
            P(None, ("kv", "ctx"), None),
            P(),
        ),
        out_specs=P(None, "ctx"),
        check_vma=False,
    )
```

```python
import functools

import jax
import jax.numpy as jnp
from jax import lax
from jax.experimental import pallas as pl
from jax.experimental.pallas import tpu as pltpu
from jax.sharding import PartitionSpec as P

D = 8192
FF = 16384
HEAD = 128
SLOTS = 512
NEG = -1e30
LOG2E = 1.4426950408889634
EPS = 1e-05
MESH = pl.DeviceIdType.MESH
f32, bf16, i32 = jnp.float32, jnp.bfloat16, jnp.int32
ORDER = (2, 1, 3)
NEAR = (1, 3, 2)


def dot(a, b, dims=((1,), (0,))):
    return lax.dot_general(a, b, (dims, ((), ())), preferred_element_type=f32)


def mult(v, n):
    return pl.multiple_of(v, n)


def lanes():
    return lax.broadcasted_iota(i32, (32, 128), 1)


def split(st):
    hi = st.astype(bf16).astype(f32)
    mid = (st - hi).astype(bf16).astype(f32)
    lo = st - hi - mid
    lane = lanes()
    return jnp.where(
        lane < 32, hi, jnp.where(lane < 64, mid, jnp.where(lane < 96, lo, 0.0))
    ).astype(bf16)


def join(block):
    v = block.astype(f32)
    v = v + pltpu.roll(v, 32, 1)
    return v + pltpu.roll(v, 64, 1)


def blend(stats):
    top = functools.reduce(jnp.maximum, stats)
    parts = [jnp.exp(s - top) for s in stats]
    total = functools.reduce(jnp.add, parts)
    inverse = 1.0 / total
    return [w * inverse for w in parts], top + jnp.log(total)


def mixed_of(factors, blocks, k):
    terms = [f[:, k : k + 1] * b for f, b in zip(factors, blocks)]
    return functools.reduce(jnp.add, terms)


def layer(
    ids_h, mask_h, lens_h, dsc_h, res_h, q_h, dk_h, dv_h, ck_h, cv_h, wo_h, so_h, gain_h,
    wg_h, wu_h, wd_h, sg_h, su_h, sd_h,
    out_ref,
    lens, dsc, ids, mask, qraw, qs, kc, vc, dk, dv, vis, pm, pt, wo, so, wg, wu, wd, sg, su, sd, ro, rg, ru, rd,
    rres, gains, acs, acr, a1s, a1r, a2s, a2r, ab, yb, hid, his, gb, ss,
    e1o, e1s, e1r, e3s, e3r,
    ls, sem_s, w_s, c_r, a1_r, a2_r, r_r, w_r, b_r, y_r, d_r, n_r, h_r, e1_r, e3_r,
):
    kv, ctx = lax.axis_index("kv"), lax.axis_index("ctx")
    c = ctx % 2
    yh = (ctx // 2) % 2
    x = (ctx // 4) % 4
    z = ctx // 16
    p = z + c * (x - z)
    q = x + c * (z - x)
    sp, sq = 16 - 12 * c, 4 + 12 * c
    yi = yh * 2 + kv
    oc = 1 - c

    core = (kv, ctx + 1 - 2 * c)

    def across(dev):
        return (dev[0], dev[1] + 1 - 2 * c)

    def p_dev(d):
        return (kv, ctx + ((p + d) % 4 - p) * sp)

    def q_dev(d):
        return (kv, ctx + ((q + d) % 4 - q) * sq)

    def y_dev(d):
        to = (yi + d) % 4
        return (to % 2, ctx + (to // 2 - yh) * 2)

    def pq_dev(d, e):
        return (kv, p_dev(d)[1] + q_dev(e)[1] - ctx)

    def qy_dev(d, e):
        return (kv, q_dev(d)[1] + e * (2 - 4 * yh))

    near_step = 3 - 2 * (yi % 2)
    near = y_dev(near_step)

    barrier = pltpu.get_barrier_semaphore()
    peers = [core] + [p_dev(d) for d in NEAR] + [q_dev(d) for d in NEAR] + [y_dev(d) for d in NEAR]
    peers += [qy_dev(d, 1) for d in NEAR]
    peers += [pq_dev(d, e) for d in NEAR for e in NEAR]
    peers += [across(y_dev(d)) for d in NEAR]
    def load(n, src, dst):
        copy = pltpu.make_async_copy(src, dst, ls.at[n])
        copy.start()
        return copy

    first = [load(0, ids_h, ids), load(1, q_h, qraw), load(17, lens_h, lens), load(18, dsc_h, dsc)]
    for peer in peers:
        pl.semaphore_signal(barrier, inc=1, device_id=peer, device_id_type=MESH)
    load(2, ck_h.at[oc], kc.at[oc])
    load(2, cv_h.at[oc], vc.at[oc])
    load(3, ck_h.at[c], kc.at[c])
    load(3, cv_h.at[c], vc.at[c])
    small = [
        load(4, mask_h, mask), load(5, dk_h, dk), load(6, dv_h, dv),
        load(7, res_h, rres.at[yh, c]), load(8, gain_h, gains.at[yh, c]),
    ]

    big, tiny = [0], [0]

    def send(src, dst, r_sem, to, s_sem=None):
        if s_sem is None:
            size = 1
            for n in src.shape:
                size *= n
            small_one = src.dtype == f32
            (tiny if small_one else big)[0] += size * (4 if small_one else 2)
            s_sem = sem_s.at[1 if small_one else 0]
        pltpu.make_async_remote_copy(
            src_ref=src, dst_ref=dst, send_sem=s_sem, recv_sem=r_sem,
            device_id=to, device_id_type=MESH,
        ).start()

    def arrived(dst, sem):
        pltpu.make_async_copy(dst, dst, sem).wait()

    for copy in first:
        copy.wait()
    row = jnp.broadcast_to(ids[...].astype(f32), (64, 64))
    ii = lax.broadcasted_iota(i32, (64, 64), 0)
    jj = lax.broadcasted_iota(i32, (64, 64), 1)
    col = jnp.sum(jnp.where(ii == jj, row, 0.0), axis=1, keepdims=True)
    same = jnp.where(row == col, 1.0, 0.0)
    pos_col = jnp.sum(jnp.where(jj < ii, same, 0.0), axis=1, keepdims=True) + 32.0 * col
    pos_row = jnp.sum(jnp.where(ii < jj, same, 0.0), axis=0, keepdims=True) + 32.0 * row[:1]
    pt[...] = jnp.where(pos_col == jj.astype(f32), 1.0, 0.0).astype(bf16)
    pm[...] = jnp.where(pos_row == ii.astype(f32), 1.0, 0.0).astype(bf16)

    for n in range(4):
        at = pl.ds(n * 1024, 1024)
        qs[:, at] = dot(pm[...], qraw[:, at]).astype(bf16)

    factor = HEAD ** (-0.5)
    c32, o32 = mult(c * 32, 32), mult(oc * 32, 32)
    first_slot = ctx * SLOTS

    def attend(t, t32, g):
        rows = jnp.concatenate(
            [qs[pl.ds(t32, 32), pl.ds(mult((g * 8 + k) * 128, 128), 128)] for k in range(8)], axis=0
        )
        at = pl.ds(mult(g * 128, 128), 128)
        s = dot(rows, kc[t, :, at], ((1,), (1,)))
        live = lax.broadcasted_iota(i32, (1, SLOTS), 1) + first_slot < lens[t]
        s = jnp.where(live, s, NEG)
        m = jnp.max(s, axis=1, keepdims=True)
        m = jnp.where(m > 0.5 * NEG, m, 0.0)
        e = jnp.exp2((s - m) * (factor * LOG2E))
        l = jnp.sum(e, axis=1, keepdims=True)
        o = dot(e.astype(bf16), vc[t, :, at])
        some = l > 0.0
        safe = jnp.where(some, l, 1.0)
        o = o * (1.0 / safe)
        lse = jnp.where(some, m * factor + jnp.log(safe), NEG)
        lane = lanes() % 32
        st = jnp.zeros((32, 128), f32)
        for k in range(8):
            st = jnp.where(lane == k, lse[k * 32 : (k + 1) * 32], st)
        return o, st

    arrived(kc, ls.at[2])
    group = [
        (wo_h, wo, so_h, so, ro, 0, D), (wg_h, wg, sg_h, sg, rg, 1, D),
        (wu_h, wu, su_h, su, ru, 2, D), (wd_h, wd, sd_h, sd, rd, 3, FF),
    ]
    rest = [
        (load(9 + 2 * n, one[0], one[1]), load(10 + 2 * n, one[2], one[3]))
        for n, one in enumerate(group)
    ]

    def combine(n):
        _, base_w, _, both, remote, at_scale, width = group[n]
        for copy in rest[n]:
            copy.wait()
        scales = [dsc[t, at_scale] * width ** (-0.5) for t in range(2)]
        count, piece = (base_w.shape[0], 256) if n < 3 else (base_w.shape[1], 256)

        @pl.loop(0, count // piece)
        def _(i):
            part = pl.ds(mult(i * piece, piece), piece)
            at = (part, slice(None)) if n < 3 else (slice(None), part)
            base_part = base_w[at].astype(f32)
            for t in range(2):
                total_part = base_part + scales[t] * both[(t, *at)].astype(f32)
                both[(t, *at)] = total_part.astype(bf16)

        send(both.at[oc], remote, w_r.at[n], core, w_s.at[n])

    def other_block(d):
        o, st = attend(oc, o32, (q + d) % 4)
        for k in range(8):
            acs[d, k] = o[k * 32 : (k + 1) * 32].astype(bf16)
        acs[d, 8] = split(st)

    def other_send(d):
        send(acs.at[d], acr.at[d], c_r.at[d], core)

    for d in ORDER + (0,):
        other_block(d)
    pl.semaphore_wait(barrier, len(peers))
    for d in ORDER + (0,):
        other_send(d)
    arrived(kc, ls.at[3])
    for copy in small:
        copy.wait()
    for n, to in enumerate((near, core, across(near))):
        send(rres.at[yh, c], rres.at[yh, c], r_r.at[0], to)
        send(gains.at[yh, c], gains.at[yh, c], r_r.at[1], to)

    def merge(d, o, st):
        factors, lse = blend([st, join(acr[d, 8])])
        for k in range(8):
            blocks = [o[k * 32 : (k + 1) * 32], acr[d, k].astype(f32)]
            a1s[d, k] = mixed_of(factors, blocks, k).astype(bf16)
        a1s[d, 8] = split(lse)
        if d:
            send(a1s.at[d], a1r.at[d - 1], a1_r.at[0], p_dev(d))

    pending = []
    for d in ORDER + (0,):
        pending.append((d, *attend(c, c32, (p + d) % 4)))
        if len(pending) > 1:
            arrived(acr.at[pending[0][0]], c_r.at[pending[0][0]])
            merge(*pending.pop(0))
    arrived(acr.at[0], c_r.at[0])
    merge(*pending.pop(0))

    vis[...] = dot(pm[...], mask[...].astype(f32).astype(bf16))
    head0 = p * 8 + q * 2
    rows = jnp.concatenate(
        [qs[pl.ds(c32, 32), pl.ds(mult((head0 + k) * 128, 128), 128)] for k in range(2)], axis=0
    )
    at_p = pl.ds(mult(p * 128, 128), 128)
    seen = jnp.concatenate([vis[pl.ds(c32, 32), :]] * 2, axis=0) > 0.5
    s = jnp.where(seen, dot(rows, dk[:, at_p], ((1,), (1,))) * factor, NEG)
    m = jnp.max(s, axis=1, keepdims=True)
    e = jnp.where(seen, jnp.exp(s - m), 0.0)
    l = jnp.sum(e, axis=1, keepdims=True)
    draft_o = dot(e.astype(bf16), dv[:, at_p]) * (1.0 / l)
    lse = m + jnp.log(l)
    draft_st = jnp.where(lanes() % 32 == 0, lse[:32], lse[32:])

    combine(0)

    arrived(a1r, a1_r.at[0])
    sources = [a1s.at[0]] + [a1r.at[n] for n in range(3)]
    factors, lse = blend([join(s[8]) for s in sources])
    keep = None
    for d in ORDER + (0,):
        to_q = (q + d) % 4
        shift = (128 - 2 * to_q) % 128
        turned = [pltpu.roll(f, shift, 1) for f in factors]
        heads = [
            mixed_of(turned, [s[2 * to_q + k].astype(f32) for s in sources], k) for k in range(2)
        ]
        st = pltpu.roll(lse, shift, 1)
        a2s[d, 0] = heads[0].astype(bf16)
        a2s[d, 1] = heads[1].astype(bf16)
        a2s[d, 2] = split(st)
        for e in (1, 0):
            if d or e:
                send(a2s.at[d], a2r.at[4 * e + d], a2_r.at[0], qy_dev(d, e))
        if not d:
            keep = (heads, st)

    others = [(0, 1), (0, 3), (1, 0), (1, 1), (1, 3), (0, 2), (1, 2)]
    combine(1)
    combine(2)
    arrived(a2r.at[pl.ds(1, 7)], a2_r.at[0])
    factors, _ = blend([keep[1]] + [join(a2r[4 * e + d, 2]) for e, d in others] + [draft_st])
    for k in range(2):
        blocks = [keep[0][k]] + [a2r[4 * e + d, k].astype(f32) for e, d in others]
        blocks.append(draft_o[k * 32 : (k + 1) * 32])
        ab[p, q, :, k * 128 : (k + 1) * 128] = mixed_of(factors, blocks, k).astype(bf16)

    def spread(buf, r_sem):
        mine = buf.at[p, q]
        for dp in (0,) + ORDER:
            for dq in ORDER + (0,):
                if dp or dq:
                    send(mine, mine, r_sem.at[dp], pq_dev(dp, dq))

    def row_in(buf, dp, r_sem):
        at_p = (p - dp + 4) % 4
        if dp:
            arrived(buf.at[at_p], r_sem.at[dp])
        else:
            arrived(buf.at[at_p, pl.ds(0, 3)], r_sem.at[0])
        return at_p

    spread(ab, b_r)
    combine(3)
    arrived(ro, w_r.at[0])
    projected = None
    for dp in (0,) + NEAR:
        at_p = row_in(ab, dp, b_r)
        lhs = jnp.concatenate([ab[at_p, n] for n in range(4)], axis=1)
        at = pl.ds(mult(at_p * 1024, 1024), 1024)
        value = dot(lhs, jnp.concatenate([so[c, at, :], ro[at, :]], axis=1))
        projected = value if projected is None else projected + value
    for n, t in ((0, c), (1, oc)):
        value = projected[:, n * 128 : (n + 1) * 128]
        yb[yi, :, pl.ds(mult(t * 128, 128), 128)] = value.astype(bf16)

    for d in ORDER:
        send(yb.at[yi], yb.at[yi], y_r.at[0], y_dev(d))
    arrived(qs.at[:, pl.ds(0, 384)], r_r.at[0])
    arrived(ss.at[pl.ds(0, 3)], r_r.at[1])
    own_rows = pm[pl.ds(c32, 32), :]
    base = [[dot(own_rows, rres[b, t]) for t in range(2)] for b in range(2)]
    arrived(yb.at[pl.ds(0, 3)], y_r.at[0])
    squares = jnp.zeros((32, 1), f32)
    for b in range(2):
        for t in range(2):
            at = slice(t * 128, (t + 1) * 128)
            h = base[b][t] + (yb[2 * b, :, at].astype(f32) + yb[2 * b + 1, :, at].astype(f32))
            his[b, t] = h
            gb[p, q, :, (2 * b + t) * 128 : (2 * b + t + 1) * 128] = (h * gains[b, t]).astype(bf16)
            squares = squares + jnp.sum(h * h, axis=1, keepdims=True)
    eye = lax.broadcasted_iota(i32, (32, 128), 0) == lanes()
    place = p * 4 + q
    ss[place] = jnp.sum(jnp.where(eye, squares, 0.0), axis=0, keepdims=True)
    for dp in ORDER + (0,):
        for dq in ORDER + (0,):
            if dp or dq:
                send(ss.at[place], ss.at[place], n_r.at[0], pq_dev(dp, dq))
    spread(gb, d_r)
    hid[c] = his[yh, c]
    send(his.at[yh, oc], hid.at[c], h_r.at[0], core, w_s.at[4])

    arrived(rg, w_r.at[1])
    arrived(ru, w_r.at[2])
    sums = [None] * 2
    for dp in (0,) + NEAR:
        at_p = row_in(gb, dp, d_r)
        if dp == 2:
            arrived(ss.at[pl.ds(0, 15)], n_r.at[0])
            whole = functools.reduce(jnp.add, [ss[n] for n in range(16)])
            total = jnp.sum(jnp.where(eye, whole, 0.0), axis=1, keepdims=True)
            scale = lax.rsqrt(total * (1.0 / D) + EPS)
        lhs = jnp.concatenate([gb[at_p, n] for n in range(4)], axis=1)

        def rows(*ref):
            parts = []
            for n in range(4):
                at = pl.ds(mult((at_p * sp + n * sq) * 128, 512), 512)
                parts.append(ref[0][(*ref[1:], at, slice(None))])
            return jnp.concatenate(parts, axis=0)

        for n, (left, right) in enumerate((((sg, c), (su, c)), ((rg,), (ru,)))):
            value = dot(lhs, jnp.concatenate([rows(*left), rows(*right)], axis=1))
            sums[n] = value if sums[n] is None else sums[n] + value

    parts = []
    for n in range(2):
        gate, up = sums[n][:, :128] * scale, sums[n][:, 128:] * scale
        parts.append((gate / (1.0 + jnp.exp(-gate)) * up).astype(bf16))
    active = jnp.concatenate(parts, axis=1)

    arrived(rd, w_r.at[3])
    for dp in ORDER + (0,):
        for dq in ORDER + (0,):
            at = pl.ds(mult(((p + dp) % 4 * sp + (q + dq) % 4 * sq) * 128, 512), 512)
            value = dot(active, jnp.concatenate([sd[c, :, at], rd[:, at]], axis=0))
            if dp or dq:
                e1s[dp, dq] = value.astype(bf16)
                send(e1s.at[dp, dq], e1r.at[4 * dp + dq], e1_r.at[0], pq_dev(dp, dq))
            else:
                e1o[...] = value
    arrived(e1r.at[pl.ds(1, 15)], e1_r.at[0])
    kept = e1o[...]
    for n in range(1, 16):
        kept = kept + e1r[n].astype(f32)
    for b in range(2):
        for t in range(2):
            at = (2 * b + t) * 128
            e3s[b, t] = kept[:, at : at + 128].astype(bf16)
    for d in ORDER + (0,):
        to_block = ((yi + d) % 4) // 2
        send(e3s.at[to_block, oc], e3r.at[c, yi], e3_r.at[0], across(y_dev(d)))
        if d:
            send(e3s.at[to_block, c], e3r.at[c, yi], e3_r.at[0], y_dev(d))
    e3r[c, yi] = e3s[yh, c]
    arrived(hid.at[oc], h_r.at[0])
    arrived(a1s.at[0, pl.ds(0, 7)], e3_r.at[0])
    results = []
    for t in range(2):
        got = [e3r[t, n].astype(f32) for n in range(4)]
        results.append((hid[t] + ((got[0] + got[1]) + (got[2] + got[3]))).astype(bf16))
    out_ref[...] = dot(pt[...], jnp.concatenate(results, axis=0)).astype(bf16)

    arrived(ss.at[pl.ds(0, tiny[0] // 512)], sem_s.at[1])
    arrived(sg.at[:, pl.ds(0, big[0] // 512)], sem_s.at[0])
    for n, one in enumerate(group):
        arrived(one[4], w_s.at[n])
    arrived(hid.at[0], w_s.at[4])


def shards(
    residual, queries, draft_keys, draft_values, cache_keys, cache_values, tenant_ids, tree_mask,
    cache_lengths, out_weight, out_signs, norm_gain, gate_weight, up_weight, down_weight,
    gate_signs, up_signs, down_signs, delta_scale,
):
    hbm = pl.BlockSpec(memory_space=pltpu.HBM)
    vm = pltpu.VMEM
    dma = pltpu.SemaphoreType.DMA
    scratch = [
        pltpu.SMEM((2,), i32), pltpu.SMEM((2, 4), f32),
        vm((1, 64), i32), vm((64, 64), i32), vm((64, 4096), bf16), vm((64, 4096), bf16),
        vm((2, SLOTS, 512), bf16), vm((2, SLOTS, 512), bf16), vm((64, 512), bf16),
        vm((64, 512), bf16), vm((64, 64), f32), vm((64, 64), bf16), vm((64, 64), bf16),
        vm((4096, 128), bf16), vm((2, 4096, 128), bf16), vm((8192, 128), bf16),
        vm((8192, 128), bf16), vm((128, 8192), bf16), vm((2, 8192, 128), bf16),
        vm((2, 8192, 128), bf16), vm((2, 128, 8192), bf16),
        vm((4096, 128), bf16), vm((8192, 128), bf16), vm((8192, 128), bf16), vm((128, 8192), bf16),
        vm((2, 2, 64, 128), bf16), vm((2, 2, 1, 128), f32),
        vm((4, 9, 32, 128), bf16), vm((4, 9, 32, 128), bf16),
        vm((4, 9, 32, 128), bf16), vm((3, 9, 32, 128), bf16),
        vm((4, 3, 32, 128), bf16), vm((8, 3, 32, 128), bf16),
        vm((4, 4, 32, 256), bf16), vm((4, 32, 256), bf16), vm((2, 32, 128), f32),
        vm((2, 2, 32, 128), f32), vm((4, 4, 32, 512), bf16), vm((20, 1, 128), f32),
        vm((32, 512), f32), vm((4, 4, 32, 512), bf16), vm((16, 32, 512), bf16),
        vm((2, 2, 32, 128), bf16), vm((2, 4, 32, 128), bf16),
        dma((19,)), dma((2,)), dma((5,)), dma((4,)), dma((1,)), dma((1,)), dma((2,)), dma((4,)),
        dma((4,)), dma((1,)), dma((4,)), dma((2,)), dma((1,)), dma((1,)), dma((1,)),
    ]
    return pl.pallas_call(
        layer,
        name="layer",
        out_shape=pltpu.VMEM((64, 128), bf16),
        in_specs=[hbm] * 19,
        out_specs=pl.BlockSpec(memory_space=pltpu.VMEM),
        scratch_shapes=scratch,
        compiler_params=pltpu.CompilerParams(
            collective_id=0, has_side_effects=True, vmem_limit_bytes=60 * 1024 * 1024
        ),
    )(
        tenant_ids.reshape(1, 64), tree_mask, cache_lengths, delta_scale, residual, queries,
        draft_keys, draft_values, cache_keys, cache_values, out_weight, out_signs,
        norm_gain.reshape(1, 128), gate_weight, up_weight, down_weight, gate_signs, up_signs,
        down_signs,
    )


def solution(mesh):
    return jax.shard_map(
        shards,
        mesh=mesh,
        in_specs=(
            P(None, "ctx"),
            P(None, "kv"),
            P(None, "kv"),
            P(None, "kv"),
            P(None, "ctx", "kv"),
            P(None, "ctx", "kv"),
            P(),
            P(),
            P(),
            P("kv", "ctx"),
            P(None, "kv", "ctx"),
            P("ctx"),
            P(None, ("kv", "ctx")),
            P(None, ("kv", "ctx")),
            P(("kv", "ctx"), None),
            P(None, None, ("kv", "ctx")),
            P(None, None, ("kv", "ctx")),
            P(None, ("kv", "ctx"), None),
            P(),
        ),
        out_specs=P(None, "ctx"),
        check_vma=False,
    )
```

```python
import functools

import jax
import jax.numpy as jnp
from jax import lax
from jax.experimental import pallas as pl
from jax.experimental.pallas import tpu as pltpu
from jax.sharding import PartitionSpec as P

D = 8192
FF = 16384
HEAD = 128
SLOTS = 512
NEG = -1e30
LOG2E = 1.4426950408889634
EPS = 1e-05
MESH = pl.DeviceIdType.MESH
f32, bf16, i32 = jnp.float32, jnp.bfloat16, jnp.int32
ORDER = (2, 1, 3)
NEAR = (1, 3, 2)


def dot(a, b, dims=((1,), (0,))):
    return lax.dot_general(a, b, (dims, ((), ())), preferred_element_type=f32)


def mult(v, n):
    return pl.multiple_of(v, n)


def lanes():
    return lax.broadcasted_iota(i32, (32, 128), 1)


def split(st):
    hi = st.astype(bf16).astype(f32)
    mid = (st - hi).astype(bf16).astype(f32)
    lo = st - hi - mid
    lane = lanes()
    return jnp.where(
        lane < 32, hi, jnp.where(lane < 64, mid, jnp.where(lane < 96, lo, 0.0))
    ).astype(bf16)


def join(block):
    v = block.astype(f32)
    v = v + pltpu.roll(v, 32, 1)
    return v + pltpu.roll(v, 64, 1)


def blend(stats):
    top = functools.reduce(jnp.maximum, stats)
    parts = [jnp.exp(s - top) for s in stats]
    total = functools.reduce(jnp.add, parts)
    inverse = 1.0 / total
    return [w * inverse for w in parts], top + jnp.log(total)


def mixed_of(factors, blocks, k):
    terms = [f[:, k : k + 1] * b for f, b in zip(factors, blocks)]
    return functools.reduce(jnp.add, terms)


def layer(
    ids_h, mask_h, lens_h, dsc_h, res_h, q_h, dk_h, dv_h, ck_h, cv_h, wo_h, so_h, gain_h,
    wg_h, wu_h, wd_h, sg_h, su_h, sd_h,
    out_ref,
    lens, dsc, ids, mask, qraw, qs, kc, vc, dk, dv, vis, pm, pt, wo, so, wg, wu, wd, sg, su, sd, ro, rg, ru, rd,
    rres, gains, acs, acr, a1s, a1r, a2s, a2r, ab, yb, hid, his, gb, ss,
    e1o, e1s, e1r, e3s, e3r,
    ls, sem_s, w_s, c_r, a1_r, a2_r, r_r, w_r, b_r, y_r, d_r, n_r, h_r, e1_r, e3_r,
):
    kv, ctx = lax.axis_index("kv"), lax.axis_index("ctx")
    c = ctx % 2
    yh = (ctx // 2) % 2
    x = (ctx // 4) % 4
    z = ctx // 16
    p = z + c * (x - z)
    q = x + c * (z - x)
    sp, sq = 16 - 12 * c, 4 + 12 * c
    yi = yh * 2 + kv
    oc = 1 - c

    core = (kv, ctx + 1 - 2 * c)

    def across(dev):
        return (dev[0], dev[1] + 1 - 2 * c)

    def p_dev(d):
        return (kv, ctx + ((p + d) % 4 - p) * sp)

    def q_dev(d):
        return (kv, ctx + ((q + d) % 4 - q) * sq)

    def y_dev(d):
        to = (yi + d) % 4
        return (to % 2, ctx + (to // 2 - yh) * 2)

    def pq_dev(d, e):
        return (kv, p_dev(d)[1] + q_dev(e)[1] - ctx)

    def qy_dev(d, e):
        return (kv, q_dev(d)[1] + e * (2 - 4 * yh))

    near_step = 3 - 2 * (yi % 2)
    near = y_dev(near_step)

    barrier = pltpu.get_barrier_semaphore()
    peers = [core] + [p_dev(d) for d in NEAR] + [q_dev(d) for d in NEAR] + [y_dev(d) for d in NEAR]
    peers += [qy_dev(d, 1) for d in NEAR]
    peers += [pq_dev(d, e) for d in NEAR for e in NEAR]
    peers += [across(y_dev(d)) for d in NEAR]
    def load(n, src, dst):
        copy = pltpu.make_async_copy(src, dst, ls.at[n])
        copy.start()
        return copy

    first = [load(0, ids_h, ids), load(1, q_h, qraw), load(17, lens_h, lens), load(18, dsc_h, dsc)]
    for peer in peers:
        pl.semaphore_signal(barrier, inc=1, device_id=peer, device_id_type=MESH)
    load(2, ck_h.at[oc], kc.at[oc])
    load(2, cv_h.at[oc], vc.at[oc])
    load(3, ck_h.at[c], kc.at[c])
    load(3, cv_h.at[c], vc.at[c])
    small = [
        load(4, mask_h, mask), load(5, dk_h, dk), load(6, dv_h, dv),
        load(7, res_h, rres.at[yh, c]), load(8, gain_h, gains.at[yh, c]),
    ]

    big, tiny = [0], [0]

    def send(src, dst, r_sem, to, s_sem=None):
        if s_sem is None:
            size = 1
            for n in src.shape:
                size *= n
            small_one = src.dtype == f32
            (tiny if small_one else big)[0] += size * (4 if small_one else 2)
            s_sem = sem_s.at[1 if small_one else 0]
        pltpu.make_async_remote_copy(
            src_ref=src, dst_ref=dst, send_sem=s_sem, recv_sem=r_sem,
            device_id=to, device_id_type=MESH,
        ).start()

    def arrived(dst, sem):
        pltpu.make_async_copy(dst, dst, sem).wait()

    for copy in first:
        copy.wait()
    row = jnp.broadcast_to(ids[...].astype(f32), (64, 64))
    ii = lax.broadcasted_iota(i32, (64, 64), 0)
    jj = lax.broadcasted_iota(i32, (64, 64), 1)
    col = jnp.sum(jnp.where(ii == jj, row, 0.0), axis=1, keepdims=True)
    same = jnp.where(row == col, 1.0, 0.0)
    pos_col = jnp.sum(jnp.where(jj < ii, same, 0.0), axis=1, keepdims=True) + 32.0 * col
    pos_row = jnp.sum(jnp.where(ii < jj, same, 0.0), axis=0, keepdims=True) + 32.0 * row[:1]
    pt[...] = jnp.where(pos_col == jj.astype(f32), 1.0, 0.0).astype(bf16)
    pm[...] = jnp.where(pos_row == ii.astype(f32), 1.0, 0.0).astype(bf16)

    for n in range(4):
        at = pl.ds(n * 1024, 1024)
        qs[:, at] = dot(pm[...], qraw[:, at]).astype(bf16)

    factor = HEAD ** (-0.5)
    c32, o32 = mult(c * 32, 32), mult(oc * 32, 32)
    first_slot = ctx * SLOTS

    def attend(t, t32, g):
        rows = jnp.concatenate(
            [qs[pl.ds(t32, 32), pl.ds(mult((g * 8 + k) * 128, 128), 128)] for k in range(8)], axis=0
        )
        at = pl.ds(mult(g * 128, 128), 128)
        s = dot(rows, kc[t, :, at], ((1,), (1,)))
        live = lax.broadcasted_iota(i32, (1, SLOTS), 1) + first_slot < lens[t]
        s = jnp.where(live, s, NEG)
        m = jnp.max(s, axis=1, keepdims=True)
        m = jnp.where(m > 0.5 * NEG, m, 0.0)
        e = jnp.exp2((s - m) * (factor * LOG2E))
        l = jnp.sum(e, axis=1, keepdims=True)
        o = dot(e.astype(bf16), vc[t, :, at])
        some = l > 0.0
        safe = jnp.where(some, l, 1.0)
        o = o * (1.0 / safe)
        lse = jnp.where(some, m * factor + jnp.log(safe), NEG)
        lane = lanes() % 32
        st = jnp.zeros((32, 128), f32)
        for k in range(8):
            st = jnp.where(lane == k, lse[k * 32 : (k + 1) * 32], st)
        return o, st

    arrived(kc, ls.at[2])
    group = [
        (wo_h, wo, so_h, so, ro, 0, D), (wg_h, wg, sg_h, sg, rg, 1, D),
        (wu_h, wu, su_h, su, ru, 2, D), (wd_h, wd, sd_h, sd, rd, 3, FF),
    ]
    rest = [
        (load(9 + 2 * n, one[0], one[1]), load(10 + 2 * n, one[2], one[3]))
        for n, one in enumerate(group)
    ]

    def combine(n):
        _, base_w, _, both, remote, at_scale, width = group[n]
        for copy in rest[n]:
            copy.wait()
        scales = [dsc[t, at_scale] * width ** (-0.5) for t in range(2)]
        count, piece = (base_w.shape[0], 256) if n < 3 else (base_w.shape[1], 256)

        @pl.loop(0, count // piece)
        def _(i):
            part = pl.ds(mult(i * piece, piece), piece)
            at = (part, slice(None)) if n < 3 else (slice(None), part)
            base_part = base_w[at].astype(f32)
            for t in range(2):
                total_part = base_part + scales[t] * both[(t, *at)].astype(f32)
                both[(t, *at)] = total_part.astype(bf16)

        send(both.at[oc], remote, w_r.at[n], core, w_s.at[n])

    def other_block(d):
        o, st = attend(oc, o32, (q + d) % 4)
        for k in range(8):
            acs[d, k] = o[k * 32 : (k + 1) * 32].astype(bf16)
        acs[d, 8] = split(st)

    def other_send(d):
        send(acs.at[d], acr.at[d], c_r.at[d], core)

    for d in ORDER + (0,):
        other_block(d)
    pl.semaphore_wait(barrier, len(peers))
    for d in ORDER + (0,):
        other_send(d)
    arrived(kc, ls.at[3])
    for copy in small:
        copy.wait()
    for n, to in enumerate((near, core, across(near))):
        send(rres.at[yh, c], rres.at[yh, c], r_r.at[0], to)
        send(gains.at[yh, c], gains.at[yh, c], r_r.at[1], to)

    def merge(d, o, st):
        factors, lse = blend([st, join(acr[d, 8])])
        for k in range(8):
            blocks = [o[k * 32 : (k + 1) * 32], acr[d, k].astype(f32)]
            a1s[d, k] = mixed_of(factors, blocks, k).astype(bf16)
        a1s[d, 8] = split(lse)
        if d:
            send(a1s.at[d], a1r.at[d - 1], a1_r.at[0], p_dev(d))

    pending = []
    for d in ORDER + (0,):
        pending.append((d, *attend(c, c32, (p + d) % 4)))
        if len(pending) > 1:
            arrived(acr.at[pending[0][0]], c_r.at[pending[0][0]])
            merge(*pending.pop(0))
    arrived(acr.at[0], c_r.at[0])
    merge(*pending.pop(0))

    vis[...] = dot(pm[...], mask[...].astype(f32).astype(bf16))
    head0 = p * 8 + q * 2
    rows = jnp.concatenate(
        [qs[pl.ds(c32, 32), pl.ds(mult((head0 + k) * 128, 128), 128)] for k in range(2)], axis=0
    )
    at_p = pl.ds(mult(p * 128, 128), 128)
    seen = jnp.concatenate([vis[pl.ds(c32, 32), :]] * 2, axis=0) > 0.5
    s = jnp.where(seen, dot(rows, dk[:, at_p], ((1,), (1,))) * factor, NEG)
    m = jnp.max(s, axis=1, keepdims=True)
    e = jnp.where(seen, jnp.exp(s - m), 0.0)
    l = jnp.sum(e, axis=1, keepdims=True)
    draft_o = dot(e.astype(bf16), dv[:, at_p]) * (1.0 / l)
    lse = m + jnp.log(l)
    draft_st = jnp.where(lanes() % 32 == 0, lse[:32], lse[32:])

    combine(0)

    arrived(a1r, a1_r.at[0])
    sources = [a1s.at[0]] + [a1r.at[n] for n in range(3)]
    factors, lse = blend([join(s[8]) for s in sources])
    keep = None
    for d in ORDER + (0,):
        to_q = (q + d) % 4
        shift = (128 - 2 * to_q) % 128
        turned = [pltpu.roll(f, shift, 1) for f in factors]
        heads = [
            mixed_of(turned, [s[2 * to_q + k].astype(f32) for s in sources], k) for k in range(2)
        ]
        st = pltpu.roll(lse, shift, 1)
        a2s[d, 0] = heads[0].astype(bf16)
        a2s[d, 1] = heads[1].astype(bf16)
        a2s[d, 2] = split(st)
        for e in (1, 0):
            if d or e:
                send(a2s.at[d], a2r.at[4 * e + d], a2_r.at[0], qy_dev(d, e))
        if not d:
            keep = (heads, st)

    others = [(0, 1), (0, 3), (1, 0), (1, 1), (1, 3), (0, 2), (1, 2)]
    combine(1)
    combine(2)
    arrived(a2r.at[pl.ds(1, 7)], a2_r.at[0])
    factors, _ = blend([keep[1]] + [join(a2r[4 * e + d, 2]) for e, d in others] + [draft_st])
    for k in range(2):
        blocks = [keep[0][k]] + [a2r[4 * e + d, k].astype(f32) for e, d in others]
        blocks.append(draft_o[k * 32 : (k + 1) * 32])
        ab[p, q, :, k * 128 : (k + 1) * 128] = mixed_of(factors, blocks, k).astype(bf16)

    def spread(buf, r_sem):
        mine = buf.at[p, q]
        far_first = sorted(
            ((a, b) for a in range(4) for b in range(4) if a or b),
            key=lambda v: (-min(v[0], 4 - v[0]) - min(v[1], 4 - v[1]), v),
        )
        for dp, dq in far_first:
            send(mine, mine, r_sem.at[dp], pq_dev(dp, dq))

    def row_in(buf, dp, r_sem):
        at_p = (p - dp + 4) % 4
        if dp:
            arrived(buf.at[at_p], r_sem.at[dp])
        else:
            arrived(buf.at[at_p, pl.ds(0, 3)], r_sem.at[0])
        return at_p

    spread(ab, b_r)
    combine(3)
    arrived(ro, w_r.at[0])
    projected = None
    for dp in (0,) + NEAR:
        at_p = row_in(ab, dp, b_r)
        lhs = jnp.concatenate([ab[at_p, n] for n in range(4)], axis=1)
        at = pl.ds(mult(at_p * 1024, 1024), 1024)
        value = dot(lhs, jnp.concatenate([so[c, at, :], ro[at, :]], axis=1))
        projected = value if projected is None else projected + value
    for n, t in ((0, c), (1, oc)):
        value = projected[:, n * 128 : (n + 1) * 128]
        yb[yi, :, pl.ds(mult(t * 128, 128), 128)] = value.astype(bf16)

    for d in ORDER:
        send(yb.at[yi], yb.at[yi], y_r.at[0], y_dev(d))
    arrived(qs.at[:, pl.ds(0, 384)], r_r.at[0])
    arrived(ss.at[pl.ds(0, 3)], r_r.at[1])
    own_rows = pm[pl.ds(c32, 32), :]
    base = [[dot(own_rows, rres[b, t]) for t in range(2)] for b in range(2)]
    arrived(yb.at[pl.ds(0, 3)], y_r.at[0])
    squares = jnp.zeros((32, 1), f32)
    for b in range(2):
        for t in range(2):
            at = slice(t * 128, (t + 1) * 128)
            h = base[b][t] + (yb[2 * b, :, at].astype(f32) + yb[2 * b + 1, :, at].astype(f32))
            his[b, t] = h
            gb[p, q, :, (2 * b + t) * 128 : (2 * b + t + 1) * 128] = (h * gains[b, t]).astype(bf16)
            squares = squares + jnp.sum(h * h, axis=1, keepdims=True)
    eye = lax.broadcasted_iota(i32, (32, 128), 0) == lanes()
    place = p * 4 + q
    ss[place] = jnp.sum(jnp.where(eye, squares, 0.0), axis=0, keepdims=True)
    for dp in ORDER + (0,):
        for dq in ORDER + (0,):
            if dp or dq:
                send(ss.at[place], ss.at[place], n_r.at[0], pq_dev(dp, dq))
    spread(gb, d_r)
    hid[c] = his[yh, c]
    send(his.at[yh, oc], hid.at[c], h_r.at[0], core, w_s.at[4])

    arrived(rg, w_r.at[1])
    arrived(ru, w_r.at[2])
    sums = [None] * 2
    for dp in (0,) + NEAR:
        at_p = row_in(gb, dp, d_r)
        if dp == 2:
            arrived(ss.at[pl.ds(0, 15)], n_r.at[0])
            whole = functools.reduce(jnp.add, [ss[n] for n in range(16)])
            total = jnp.sum(jnp.where(eye, whole, 0.0), axis=1, keepdims=True)
            scale = lax.rsqrt(total * (1.0 / D) + EPS)
        lhs = jnp.concatenate([gb[at_p, n] for n in range(4)], axis=1)

        def rows(*ref):
            parts = []
            for n in range(4):
                at = pl.ds(mult((at_p * sp + n * sq) * 128, 512), 512)
                parts.append(ref[0][(*ref[1:], at, slice(None))])
            return jnp.concatenate(parts, axis=0)

        for n, (left, right) in enumerate((((sg, c), (su, c)), ((rg,), (ru,)))):
            value = dot(lhs, jnp.concatenate([rows(*left), rows(*right)], axis=1))
            sums[n] = value if sums[n] is None else sums[n] + value

    parts = []
    for n in range(2):
        gate, up = sums[n][:, :128] * scale, sums[n][:, 128:] * scale
        parts.append((gate / (1.0 + jnp.exp(-gate)) * up).astype(bf16))
    active = jnp.concatenate(parts, axis=1)

    arrived(rd, w_r.at[3])
    for dp in ORDER + (0,):
        for dq in ORDER + (0,):
            at = pl.ds(mult(((p + dp) % 4 * sp + (q + dq) % 4 * sq) * 128, 512), 512)
            value = dot(active, jnp.concatenate([sd[c, :, at], rd[:, at]], axis=0))
            if dp or dq:
                e1s[dp, dq] = value.astype(bf16)
                send(e1s.at[dp, dq], e1r.at[4 * dp + dq], e1_r.at[0], pq_dev(dp, dq))
            else:
                e1o[...] = value
    arrived(e1r.at[pl.ds(1, 15)], e1_r.at[0])
    kept = e1o[...]
    for n in range(1, 16):
        kept = kept + e1r[n].astype(f32)
    for b in range(2):
        for t in range(2):
            at = (2 * b + t) * 128
            e3s[b, t] = kept[:, at : at + 128].astype(bf16)
    for d in ORDER + (0,):
        to_block = ((yi + d) % 4) // 2
        send(e3s.at[to_block, oc], e3r.at[c, yi], e3_r.at[0], across(y_dev(d)))
        if d:
            send(e3s.at[to_block, c], e3r.at[c, yi], e3_r.at[0], y_dev(d))
    e3r[c, yi] = e3s[yh, c]
    arrived(hid.at[oc], h_r.at[0])
    arrived(a1s.at[0, pl.ds(0, 7)], e3_r.at[0])
    results = []
    for t in range(2):
        got = [e3r[t, n].astype(f32) for n in range(4)]
        results.append((hid[t] + ((got[0] + got[1]) + (got[2] + got[3]))).astype(bf16))
    out_ref[...] = dot(pt[...], jnp.concatenate(results, axis=0)).astype(bf16)

    arrived(ss.at[pl.ds(0, tiny[0] // 512)], sem_s.at[1])
    arrived(sg.at[:, pl.ds(0, big[0] // 512)], sem_s.at[0])
    for n, one in enumerate(group):
        arrived(one[4], w_s.at[n])
    arrived(hid.at[0], w_s.at[4])


def shards(
    residual, queries, draft_keys, draft_values, cache_keys, cache_values, tenant_ids, tree_mask,
    cache_lengths, out_weight, out_signs, norm_gain, gate_weight, up_weight, down_weight,
    gate_signs, up_signs, down_signs, delta_scale,
):
    hbm = pl.BlockSpec(memory_space=pltpu.HBM)
    vm = pltpu.VMEM
    dma = pltpu.SemaphoreType.DMA
    scratch = [
        pltpu.SMEM((2,), i32), pltpu.SMEM((2, 4), f32),
        vm((1, 64), i32), vm((64, 64), i32), vm((64, 4096), bf16), vm((64, 4096), bf16),
        vm((2, SLOTS, 512), bf16), vm((2, SLOTS, 512), bf16), vm((64, 512), bf16),
        vm((64, 512), bf16), vm((64, 64), f32), vm((64, 64), bf16), vm((64, 64), bf16),
        vm((4096, 128), bf16), vm((2, 4096, 128), bf16), vm((8192, 128), bf16),
        vm((8192, 128), bf16), vm((128, 8192), bf16), vm((2, 8192, 128), bf16),
        vm((2, 8192, 128), bf16), vm((2, 128, 8192), bf16),
        vm((4096, 128), bf16), vm((8192, 128), bf16), vm((8192, 128), bf16), vm((128, 8192), bf16),
        vm((2, 2, 64, 128), bf16), vm((2, 2, 1, 128), f32),
        vm((4, 9, 32, 128), bf16), vm((4, 9, 32, 128), bf16),
        vm((4, 9, 32, 128), bf16), vm((3, 9, 32, 128), bf16),
        vm((4, 3, 32, 128), bf16), vm((8, 3, 32, 128), bf16),
        vm((4, 4, 32, 256), bf16), vm((4, 32, 256), bf16), vm((2, 32, 128), f32),
        vm((2, 2, 32, 128), f32), vm((4, 4, 32, 512), bf16), vm((20, 1, 128), f32),
        vm((32, 512), f32), vm((4, 4, 32, 512), bf16), vm((16, 32, 512), bf16),
        vm((2, 2, 32, 128), bf16), vm((2, 4, 32, 128), bf16),
        dma((19,)), dma((2,)), dma((5,)), dma((4,)), dma((1,)), dma((1,)), dma((2,)), dma((4,)),
        dma((4,)), dma((1,)), dma((4,)), dma((2,)), dma((1,)), dma((1,)), dma((1,)),
    ]
    return pl.pallas_call(
        layer,
        name="layer",
        out_shape=pltpu.VMEM((64, 128), bf16),
        in_specs=[hbm] * 19,
        out_specs=pl.BlockSpec(memory_space=pltpu.VMEM),
        scratch_shapes=scratch,
        compiler_params=pltpu.CompilerParams(
            collective_id=0, has_side_effects=True, vmem_limit_bytes=60 * 1024 * 1024
        ),
    )(
        tenant_ids.reshape(1, 64), tree_mask, cache_lengths, delta_scale, residual, queries,
        draft_keys, draft_values, cache_keys, cache_values, out_weight, out_signs,
        norm_gain.reshape(1, 128), gate_weight, up_weight, down_weight, gate_signs, up_signs,
        down_signs,
    )


def solution(mesh):
    return jax.shard_map(
        shards,
        mesh=mesh,
        in_specs=(
            P(None, "ctx"),
            P(None, "kv"),
            P(None, "kv"),
            P(None, "kv"),
            P(None, "ctx", "kv"),
            P(None, "ctx", "kv"),
            P(),
            P(),
            P(),
            P("kv", "ctx"),
            P(None, "kv", "ctx"),
            P("ctx"),
            P(None, ("kv", "ctx")),
            P(None, ("kv", "ctx")),
            P(("kv", "ctx"), None),
            P(None, None, ("kv", "ctx")),
            P(None, None, ("kv", "ctx")),
            P(None, ("kv", "ctx"), None),
            P(),
        ),
        out_specs=P(None, "ctx"),
        check_vma=False,
    )
```
